256 devices in a mesh: pp: 8 (over z_lo, y), ep: 32 (over x, z_hi, core).
Axes of the slice: x: 4, y: 4, z: 8 (z_hi: 4, z_lo: 2; z = z_hi * 2 + z_lo), core: 2. Of those that a mesh axis runs over, the one named last changes fastest.
Arguments:
- fwd_tokens: bfloat16 [8, 4096, 4096], P('pp', 'ep'), may hold values from -6 to 6
- fwd_routes: int32 [8, 4096, 1], P('pp', 'ep'), may hold values from 0 to 7; in each aligned block of 128 rows (0 to 127, 128 to 255, ..., all dimensions but the last counted through in order) at most 24 rows name the same one
- fwd_gates: float32 [8, 4096, 1], P('pp', 'ep'), may hold values from 0.05 to 0.6
- bwd_tokens: bfloat16 [8, 4096, 4096], P('pp', 'ep'), may hold values from -6 to 6
- bwd_grads: bfloat16 [8, 4096, 4096], P('pp', 'ep'), may hold values from -6 to 6
- bwd_routes: int32 [8, 4096, 1], P('pp', 'ep'), may hold values from 0 to 7; in each aligned block of 128 rows (0 to 127, 128 to 255, ..., all dimensions but the last counted through in order) at most 24 rows name the same one
- bwd_gates: float32 [8, 4096, 1], P('pp', 'ep'), may hold values from 0.05 to 0.6
- gate_proj: bfloat16 [8, 32, 1024, 768], P('pp', 'ep'), may hold values from -0.09375 to 0.09375
- up_proj: bfloat16 [8, 32, 1024, 768], P('pp', 'ep'), may hold values from -0.09375 to 0.09375
- down_proj: bfloat16 [8, 32, 768, 1024], P('pp', 'ep'), may hold values from -0.21875 to 0.21875
Outputs:
- handed_forward: bfloat16 [8, 4096, 4096], P('pp', 'ep')
- handed_backward: bfloat16 [8, 4096, 4096], P('pp', 'ep')
The draws below stay inside these ranges and needn't reach their ends.
Inputs may be any that keep to these rules, and one draw needn't show every extreme that they name: `fwd_routes`: among the 128 tokens of one index of ep, no expert is named by more than 24 tokens, and in some such block an expert is named exactly 24 times. `bwd_routes`: among the 128 tokens of one index of ep, no expert is named by more than 24 tokens, and in some such block an expert is named exactly 24 times.
All inputs are finite; a program needn't handle non-finite values.
Results may differ from the reference program's by a relative error of at most 0.0071.
Values may be sent and summed in bfloat16 or wider, within the bound.
A program may use at most 128 MiB of HBM per device.

```python
import math
import jax
import jax.numpy as jnp
import numpy as np
from jax import lax

D = 4096
FF = 768
TOPW = 1
TD = 128
EXP_WIN = 8
CAP = 24
TOKENS = 4096
N_PP = 8
N_EP = 32


def shard_levels(stream_key, dims, pieces, least, high):
    loudness = 1.0
    for axis_at, shards_of in pieces:
        draws = jax.random.uniform(jax.random.fold_in(jax.random.fold_in(stream_key, 6), axis_at), (shards_of,), jnp.float32, least / len(pieces), high / len(pieces))
        loudness = loudness * jnp.repeat(jnp.exp(draws), dims[axis_at] // shards_of).reshape((-1,) + (1,) * (len(dims) - 1 - axis_at))
    return loudness


def routed_block(rng, own, number, rows, count, top, most, skew):
    ranking = jax.random.permutation(rng, count)
    heavy_load, common = load_shares(count, rows * top, most, skew, True), load_shares(count, rows * top, most, skew, False)
    places = jnp.arange(count)

    def named(lengths, turn):
        used = int((lengths > 0).sum())
        fixed = max(1, used // 4)
        moved = fixed + (places - fixed + turn * (used - fixed)) % max(1, count - fixed)
        return jnp.zeros((count,), jnp.int32).at[ranking[jnp.where(places < fixed, places, moved)]].set(jnp.asarray(lengths, jnp.int32))

    lengths = jnp.where(number % 4 == 0, named(heavy_load, number // 4), named(common, number - number // 4 - 1))
    mixed = jax.random.permutation(jax.random.fold_in(own, 3), count)
    giver, taker = mixed[0:count // 2 * 2:2], mixed[1:count // 2 * 2:2]
    room = jnp.minimum(lengths[giver] - 1, most - lengths[taker]) // 2
    room = jnp.where((giver == ranking[0]) | (taker == ranking[0]) | (lengths[taker] == 0), 0, jnp.maximum(room, 0))
    moved = jax.random.randint(jax.random.fold_in(own, 4), (count // 2,), 0, 1 << 20) % (room + 1)
    lengths = lengths.at[giver].add(-moved).at[taker].add(moved)
    labels = jnp.searchsorted(jnp.cumsum(lengths), jnp.arange(rows * top), side="right").astype(jnp.int32)
    grid = labels.reshape(top, rows).T
    grid = grid[jax.random.permutation(jax.random.fold_in(own, 1), rows)]
    turn = jax.random.randint(jax.random.fold_in(own, 2), (rows, 1), 0, top)
    return jnp.take_along_axis(grid, (jnp.arange(top)[None, :] + turn) % top, axis=1)


def load_shares(count, total, limit, lean, full):
    weights = [(1 << 20) // math.isqrt(grade ** lean) + 1 for grade in range(1, count + 1)]
    largest = limit if full else min(limit, max(-(-total // count), total * weights[0] // sum(weights)))
    least = 1 if total - largest >= count - 1 else 0
    counts, surplus = [largest] + [least] * (count - 1), total - largest - least * (count - 1)
    while surplus > 0:
        candidates = [i for i in range(1, count) if counts[i] < largest] or [i for i in range(1, count) if counts[i] < limit]
        whole, budget = sum([weights[i] for i in candidates]), surplus
        for i in candidates:
            extra = min(limit - counts[i], max(1, budget * weights[i] // whole), surplus)
            counts[i] = counts[i] + extra
            surplus = surplus - extra
    return np.array(counts)


def normal_values(stream_key, shape, width, limit, cuts=(), kind=jnp.bfloat16):
    factor_of = shard_levels(stream_key, shape, cuts, -0.22, 0.18) if cuts else 1.0
    values = jax.random.normal(stream_key, shape, jnp.float32) * width * factor_of
    return jnp.minimum(jnp.maximum(values, -limit), limit).astype(kind)


def setup_inputs(seed: int = 0) -> dict:
    seeds = jax.random.split(jax.random.key(seed), 11)
    fwd_tokens = normal_values(seeds[0], (N_PP, TOKENS, D), 1.0, 6.0, ((0, 8), (1, 32)))
    fwd_routes_keys = jax.random.split(jax.random.fold_in(seeds[1], 1), N_PP * TOKENS // TD)
    fwd_routes_turns = jax.random.permutation(jax.random.fold_in(seeds[1], 3), N_PP * TOKENS // TD)
    fwd_routes = jax.vmap(lambda own, number: routed_block(jax.random.fold_in(seeds[1], 2), own, number, TD, EXP_WIN, TOPW, CAP, 2))(fwd_routes_keys, fwd_routes_turns).reshape((N_PP, TOKENS, TOPW))
    fwd_gates = jnp.clip(jnp.exp(math.log(0.6) - 2.4849067 * jax.random.uniform(seeds[2], (N_PP, TOKENS, TOPW), jnp.float32) ** shard_levels(seeds[2], (N_PP, TOKENS, TOPW), ((0, 8), (1, 32)), -0.2, 0.2)), 0.05, 0.6)
    bwd_tokens = normal_values(seeds[3], (N_PP, TOKENS, D), 1.0, 6.0, ((0, 8), (1, 32)))
    bwd_grads = normal_values(seeds[4], (N_PP, TOKENS, D), 1.0, 6.0, ((0, 8), (1, 32)))
    bwd_routes_keys = jax.random.split(jax.random.fold_in(seeds[5], 1), N_PP * TOKENS // TD)
    bwd_routes_turns = jax.random.permutation(jax.random.fold_in(seeds[5], 3), N_PP * TOKENS // TD)
    bwd_routes = jax.vmap(lambda own, number: routed_block(jax.random.fold_in(seeds[5], 2), own, number, TD, EXP_WIN, TOPW, CAP, 2))(bwd_routes_keys, bwd_routes_turns).reshape((N_PP, TOKENS, TOPW))
    bwd_gates = jnp.clip(jnp.exp(math.log(0.6) - 2.4849067 * jax.random.uniform(seeds[6], (N_PP, TOKENS, TOPW), jnp.float32) ** shard_levels(seeds[6], (N_PP, TOKENS, TOPW), ((0, 8), (1, 32)), -0.2, 0.2)), 0.05, 0.6)
    gate_proj = normal_values(seeds[7], (N_PP, 4 * EXP_WIN, D // 4, FF), D ** -0.5, 0.09375, ((0, 8), (1, 32)))
    up_proj = normal_values(seeds[8], (N_PP, 4 * EXP_WIN, D // 4, FF), D ** -0.5, 0.09375, ((0, 8), (1, 32)))
    down_proj = normal_values(seeds[9], (N_PP, 4 * EXP_WIN, FF, D // 4), FF ** -0.5, 0.21875, ((0, 8), (1, 32)))
    return {"fwd_tokens": fwd_tokens, "fwd_routes": fwd_routes, "fwd_gates": fwd_gates, "bwd_tokens": bwd_tokens, "bwd_grads": bwd_grads, "bwd_routes": bwd_routes, "bwd_gates": bwd_gates, "gate_proj": gate_proj, "up_proj": up_proj, "down_proj": down_proj}


def slot_places(routes):
    flat_routes = routes.reshape(-1)
    onehot = (flat_routes[:, None] == jnp.arange(EXP_WIN, dtype=jnp.int32)[None, :]).astype(jnp.int32)
    before = jnp.cumsum(onehot, axis=0) - onehot
    position = jnp.sum(before * onehot, axis=1)
    slot_match = (position[:, None] == jnp.arange(CAP, dtype=jnp.int32)[None, :]).astype(jnp.float32)
    placed = onehot.astype(jnp.float32)[:, :, None] * slot_match[:, None, :]
    return placed.reshape(TD, TOPW, EXP_WIN, CAP)


def spread_rows(places, values):
    laid_out = values.astype(jnp.float32).reshape(N_EP, TD, 4, D // 4)
    return jnp.einsum("ntkec,nthf->ehncf", places, laid_out)


def device_rows(placed):
    return placed.astype(jnp.bfloat16).reshape(N_EP, N_EP * CAP, D // 4)


def both_partials(row_blocks, gate_mats, up_mats):
    def project_pair(packed):
        block, gate_mat, up_mat = packed
        gate_part = jnp.dot(block, gate_mat, preferred_element_type=jnp.float32)
        up_part = jnp.dot(block, up_mat, preferred_element_type=jnp.float32)
        return jnp.concatenate([gate_part, up_part], axis=1).astype(jnp.bfloat16)

    return lax.map(project_pair, (row_blocks, gate_mats, up_mats))


def quad_total(partials):
    shaped = partials.reshape(EXP_WIN, 4, partials.shape[1], partials.shape[2]).astype(jnp.float32)
    return shaped[:, 0] + shaped[:, 1] + shaped[:, 2] + shaped[:, 3]


def collect(places, returned):
    shaped = returned.reshape(EXP_WIN, 4, N_EP, CAP, D // 4).astype(jnp.float32)
    return jnp.einsum("ntkec,ehncf->ntkhf", places, shaped)


def down_apply(packed):
    hidden_block, down_mat = packed
    return jnp.dot(hidden_block, down_mat, preferred_element_type=jnp.float32).astype(jnp.bfloat16)


def down_back(packed):
    grad_block, down_mat = packed
    return jnp.dot(grad_block, down_mat.T, preferred_element_type=jnp.float32).astype(jnp.bfloat16)


def input_back(packed):
    gate_grad, up_grad, gate_mat, up_mat = packed
    summed = jnp.dot(gate_grad, gate_mat.T, preferred_element_type=jnp.float32)
    summed = summed + jnp.dot(up_grad, up_mat.T, preferred_element_type=jnp.float32)
    return summed.astype(jnp.bfloat16)


def section_step(packed):
    (fwd_x, fwd_r, fwd_g, bwd_x, bwd_dy, bwd_r, bwd_g, gate_mats, up_mats, down_mats) = packed
    places_fwd = jax.vmap(slot_places)(fwd_r.reshape(N_EP, TD, TOPW))
    places_bwd = jax.vmap(slot_places)(bwd_r.reshape(N_EP, TD, TOPW))

    rows_fwd = device_rows(spread_rows(places_fwd, fwd_x))
    sum_fwd = quad_total(both_partials(rows_fwd, gate_mats, up_mats))
    hidden_fwd = (jax.nn.silu(sum_fwd[:, :, :FF]) * sum_fwd[:, :, FF:]).astype(jnp.bfloat16)
    expert_out = lax.map(down_apply, (jnp.repeat(hidden_fwd, 4, axis=0), down_mats))
    gathered = collect(places_fwd, expert_out)
    weights_fwd = fwd_g.reshape(N_EP, TD, TOPW)[:, :, :, None, None]
    mixture = jnp.sum(gathered * weights_fwd, axis=2).reshape(TOKENS, D).astype(jnp.bfloat16)

    slot_gate = jnp.einsum("ntkec,ntk->nec", places_bwd, bwd_g.reshape(N_EP, TD, TOPW))
    slot_scale = jnp.transpose(slot_gate, (1, 0, 2))[:, None, :, :, None]
    rows_bwd = device_rows(spread_rows(places_bwd, bwd_x))
    grads_bwd = device_rows(spread_rows(places_bwd, bwd_dy) * slot_scale)
    sum_bwd = quad_total(both_partials(rows_bwd, gate_mats, up_mats))
    grad_hidden = quad_total(lax.map(down_back, (grads_bwd, down_mats)))
    gate_value = sum_bwd[:, :, :FF]
    up_value = sum_bwd[:, :, FF:]
    sigmoid_value = jax.nn.sigmoid(gate_value)
    grad_gate = (grad_hidden * up_value * sigmoid_value * (1.0 + gate_value * (1.0 - sigmoid_value))).astype(jnp.bfloat16)
    grad_up = (grad_hidden * gate_value * sigmoid_value).astype(jnp.bfloat16)
    grad_rows = lax.map(input_back, (jnp.repeat(grad_gate, 4, axis=0), jnp.repeat(grad_up, 4, axis=0), gate_mats, up_mats))
    grad_input = jnp.sum(collect(places_bwd, grad_rows), axis=2).reshape(TOKENS, D).astype(jnp.bfloat16)
    return mixture, grad_input


def reference(fwd_tokens, fwd_routes, fwd_gates, bwd_tokens, bwd_grads, bwd_routes, bwd_gates, gate_proj, up_proj, down_proj):
    mixture, grad_input = lax.map(section_step, (fwd_tokens, fwd_routes, fwd_gates, bwd_tokens, bwd_grads, bwd_routes, bwd_gates, gate_proj, up_proj, down_proj))
    blank_rows = jnp.zeros((1, TOKENS, D), jnp.bfloat16)
    handed_forward = jnp.concatenate([blank_rows, mixture[:-1]], axis=0)
    handed_backward = jnp.concatenate([grad_input[1:], blank_rows], axis=0)
    return (handed_forward, handed_backward)
```

```python
import jax
import jax.numpy as jnp
from jax import lax
from jax.sharding import PartitionSpec as P


def partner(block, axis, distance):
    count = lax.axis_size(axis)
    route = []
    for low in range(count):
        high = low | 1 << distance
        if high != low and high < count:
            route += [(low, high), (high, low)]
    return lax.ppermute(block, axis, route)


def shifted(shard, axis, by):
    count = lax.axis_size(axis)
    pairs = [(i, i + by) for i in range(count) if 0 <= i + by < count]
    return lax.ppermute(shard, axis, pairs)


def slot_places(routes, expert_count, slot_cap):
    tok_count = routes.shape[0]
    route_width = routes.shape[1]
    flat_routes = routes.reshape(-1)
    onehot = (flat_routes[:, None] == jnp.arange(expert_count, dtype=jnp.int32)[None, :]).astype(
        jnp.int32
    )
    before = jnp.cumsum(onehot, axis=0) - onehot
    position = jnp.sum(before * onehot, axis=1)
    slot_match = (position[:, None] == jnp.arange(slot_cap, dtype=jnp.int32)[None, :]).astype(
        jnp.float32
    )
    placed = onehot.astype(jnp.float32)[:, :, None] * slot_match[:, None, :]
    return placed.reshape(tok_count, route_width, expert_count, slot_cap)


def spread_rows(places, values):
    tok_count = values.shape[0]
    quarter_width = values.shape[1] // 4
    return jnp.einsum(
        "tkec,thf->ehcf",
        places.astype(jnp.bfloat16),
        values.reshape(tok_count, 4, quarter_width),
        preferred_element_type=jnp.float32,
    )


def device_rows(placed):
    return placed.astype(jnp.bfloat16).reshape(
        4 * placed.shape[0], placed.shape[2], placed.shape[3]
    )


def collect(places, returned):
    expert_count = places.shape[2]
    shaped = returned.reshape(expert_count, 4, returned.shape[1], returned.shape[2])
    return jnp.einsum(
        "tkec,ehcf->tkhf", places.astype(jnp.bfloat16), shaped, preferred_element_type=jnp.float32
    )


def contract_cols(left, right):
    return lax.dot_general(
        left, right, (((1,), (1,)), ((), ())), preferred_element_type=jnp.float32
    )


def quarter_bits():
    quarter = lax.axis_index("ep") % 4
    return quarter // 2, quarter % 2


def pick(flag, when_set, when_clear):
    return jnp.where(flag == 1, when_set, when_clear)


def scatter_sum(partials):
    high, low = quarter_bits()
    grouped = partials.reshape(2, 2, partials.shape[0] // 4, partials.shape[1])
    keep_half = pick(high, grouped[1], grouped[0])
    give_half = pick(high, grouped[0], grouped[1])
    pair_sum = keep_half.astype(jnp.float32) + partner(give_half, "ep", 1).astype(jnp.float32)
    keep_group = pick(low, pair_sum[1], pair_sum[0])
    give_group = pick(low, pair_sum[0], pair_sum[1])
    return keep_group + partner(give_group, "ep", 0)


def gather_groups(block):
    high, low = quarter_bits()
    pair = jnp.stack([block, partner(block, "ep", 1)])
    held = jnp.stack([pair, partner(pair, "ep", 0)], axis=1)
    held = pick(high, held[::-1], held)
    held = pick(low, held[:, ::-1], held)
    return held.reshape(-1, block.shape[1])


def forward_expert(row_block, w_gate, w_up, w_down):
    proj_width = w_gate.shape[1]
    partials = jnp.concatenate(
        [
            jnp.dot(row_block, w_gate, preferred_element_type=jnp.float32),
            jnp.dot(row_block, w_up, preferred_element_type=jnp.float32),
        ],
        axis=1,
    ).astype(jnp.bfloat16)
    summed = scatter_sum(partials)
    hidden = (jax.nn.silu(summed[:, :proj_width]) * summed[:, proj_width:]).astype(jnp.bfloat16)
    hidden = gather_groups(hidden)
    return jnp.dot(hidden, w_down, preferred_element_type=jnp.float32).astype(jnp.bfloat16)


def backward_expert(row_block, grad_block, w_gate, w_up, w_down):
    proj_width = w_gate.shape[1]
    partials = jnp.concatenate(
        [
            jnp.dot(row_block, w_gate, preferred_element_type=jnp.float32),
            jnp.dot(row_block, w_up, preferred_element_type=jnp.float32),
        ],
        axis=1,
    ).astype(jnp.bfloat16)
    grad_part = contract_cols(grad_block, w_down).astype(jnp.bfloat16)
    summed = scatter_sum(jnp.concatenate([partials, grad_part], axis=1))
    gate_value = summed[:, :proj_width]
    up_value = summed[:, proj_width : 2 * proj_width]
    grad_hidden = summed[:, 2 * proj_width :]
    sigmoid_value = jax.nn.sigmoid(gate_value)
    grad_gate = (
        grad_hidden * up_value * sigmoid_value * (1.0 + gate_value * (1.0 - sigmoid_value))
    ).astype(jnp.bfloat16)
    grad_up = (grad_hidden * gate_value * sigmoid_value).astype(jnp.bfloat16)
    grads = gather_groups(jnp.concatenate([grad_gate, grad_up], axis=1))
    result = contract_cols(grads[:, :proj_width], w_gate) + contract_cols(
        grads[:, proj_width:], w_up
    )
    return result.astype(jnp.bfloat16)


def on_device(
    fwd_tokens,
    fwd_routes,
    fwd_gates,
    bwd_tokens,
    bwd_grads,
    bwd_routes,
    bwd_gates,
    gate_proj,
    up_proj,
    down_proj,
):
    expert_count = lax.axis_size("ep") // 4
    tokens_fwd = fwd_tokens[0]
    tok_count = tokens_fwd.shape[0]
    route_width = fwd_routes.shape[2]
    slot_cap = 3 * tok_count * route_width // (2 * expert_count)
    places_fwd = slot_places(fwd_routes[0], expert_count, slot_cap)
    places_bwd = slot_places(bwd_routes[0], expert_count, slot_cap)
    send_fwd = device_rows(spread_rows(places_fwd, tokens_fwd))
    send_rows = device_rows(spread_rows(places_bwd, bwd_tokens[0]))
    slot_gate = jnp.einsum("tkec,tk->ec", places_bwd, bwd_gates[0], precision=lax.Precision.HIGHEST)
    send_grads = device_rows(spread_rows(places_bwd, bwd_grads[0]) * slot_gate[:, None, :, None])
    recv_fwd = lax.all_to_all(send_fwd, "ep", split_axis=0, concat_axis=0, tiled=True)
    recv_rows, recv_grads = (
        lax.all_to_all(send_rows, "ep", split_axis=0, concat_axis=0, tiled=True),
        lax.all_to_all(send_grads, "ep", split_axis=0, concat_axis=0, tiled=True),
    )
    quarter_width = send_fwd.shape[2]
    w_gate = gate_proj[0, 0]
    w_up = up_proj[0, 0]
    w_down = down_proj[0, 0]
    out_fwd = forward_expert(recv_fwd.reshape(-1, quarter_width), w_gate, w_up, w_down).reshape(
        recv_fwd.shape
    )
    out_bwd = backward_expert(
        recv_rows.reshape(-1, quarter_width),
        recv_grads.reshape(-1, quarter_width),
        w_gate,
        w_up,
        w_down,
    ).reshape(recv_rows.shape)
    back_fwd = lax.all_to_all(out_fwd, "ep", split_axis=0, concat_axis=0, tiled=True)
    back_bwd = lax.all_to_all(out_bwd, "ep", split_axis=0, concat_axis=0, tiled=True)
    gathered = collect(places_fwd, back_fwd)
    mixture = (
        jnp.sum(gathered * fwd_gates[0][:, :, None, None], axis=1)
        .reshape(tok_count, -1)
        .astype(jnp.bfloat16)
    )
    grad_input = (
        jnp.sum(collect(places_bwd, back_bwd), axis=1).reshape(tok_count, -1).astype(jnp.bfloat16)
    )
    handed_forward = shifted(mixture[None], "pp", 1)
    handed_backward = shifted(grad_input[None], "pp", -1)
    return (handed_forward, handed_backward)


def solution(mesh):
    return jax.shard_map(
        on_device,
        mesh=mesh,
        in_specs=(
            P("pp", "ep", None),
            P("pp", "ep", None),
            P("pp", "ep", None),
            P("pp", "ep", None),
            P("pp", "ep", None),
            P("pp", "ep", None),
            P("pp", "ep", None),
            P("pp", "ep", None, None),
            P("pp", "ep", None, None),
            P("pp", "ep", None, None),
        ),
        out_specs=(P("pp", "ep", None), P("pp", "ep", None)),
        check_vma=False,
    )
```

```python
import jax
import jax.numpy as jnp
from jax import lax
from jax.sharding import PartitionSpec as P


def partner(block, axis, distance):
    count = lax.axis_size(axis)
    route = []
    for low in range(count):
        high = low | 1 << distance
        if high != low and high < count:
            route += [(low, high), (high, low)]
    return lax.ppermute(block, axis, route)


def shifted(shard, axis, by):
    count = lax.axis_size(axis)
    pairs = [(i, i + by) for i in range(count) if 0 <= i + by < count]
    return lax.ppermute(shard, axis, pairs)


def slot_places(routes, expert_count, slot_cap):
    tok_count = routes.shape[0]
    route_width = routes.shape[1]
    flat_routes = routes.reshape(-1)
    onehot = (flat_routes[:, None] == jnp.arange(expert_count, dtype=jnp.int32)[None, :]).astype(
        jnp.int32
    )
    before = jnp.cumsum(onehot, axis=0) - onehot
    position = jnp.sum(before * onehot, axis=1)
    slot_match = (position[:, None] == jnp.arange(slot_cap, dtype=jnp.int32)[None, :]).astype(
        jnp.float32
    )
    placed = onehot.astype(jnp.float32)[:, :, None] * slot_match[:, None, :]
    return placed.reshape(tok_count, route_width, expert_count, slot_cap)


def spread_rows(places, values):
    tok_count = values.shape[0]
    quarter_width = values.shape[1] // 4
    return jnp.einsum(
        "tkec,thf->ehcf",
        places.astype(jnp.bfloat16),
        values.reshape(tok_count, 4, quarter_width),
        preferred_element_type=jnp.float32,
    )


def device_rows(placed):
    return placed.astype(jnp.bfloat16).reshape(
        4 * placed.shape[0], placed.shape[2], placed.shape[3]
    )


def collect(places, returned):
    expert_count = places.shape[2]
    shaped = returned.reshape(expert_count, 4, returned.shape[1], returned.shape[2])
    return jnp.einsum(
        "tkec,ehcf->tkhf", places.astype(jnp.bfloat16), shaped, preferred_element_type=jnp.float32
    )


def contract_cols(left, right):
    return lax.dot_general(
        left, right, (((1,), (1,)), ((), ())), preferred_element_type=jnp.float32
    )


def quarter_bits():
    quarter = lax.axis_index("ep") % 4
    return quarter // 2, quarter % 2


def pick(flag, when_set, when_clear):
    return jnp.where(flag == 1, when_set, when_clear)


def scatter_sum(partials):
    high, low = quarter_bits()
    grouped = partials.reshape(2, 2, partials.shape[0] // 4, partials.shape[1])
    keep_pair = pick(low, grouped[:, 1], grouped[:, 0])
    give_pair = pick(low, grouped[:, 0], grouped[:, 1])
    pair_sum = keep_pair.astype(jnp.float32) + partner(give_pair, "ep", 0).astype(jnp.float32)
    keep_group = pick(high, pair_sum[1], pair_sum[0])
    give_group = pick(high, pair_sum[0], pair_sum[1])
    return keep_group + partner(give_group, "ep", 1)


def gather_groups(block):
    high, low = quarter_bits()
    pair = jnp.stack([block, partner(block, "ep", 1)])
    held = jnp.stack([pair, partner(pair, "ep", 0)], axis=1)
    held = pick(high, held[::-1], held)
    held = pick(low, held[:, ::-1], held)
    return held.reshape(-1, block.shape[1])


def forward_expert(row_block, w_gate, w_up, w_down):
    proj_width = w_gate.shape[1]
    partials = jnp.concatenate(
        [
            jnp.dot(row_block, w_gate, preferred_element_type=jnp.float32),
            jnp.dot(row_block, w_up, preferred_element_type=jnp.float32),
        ],
        axis=1,
    ).astype(jnp.bfloat16)
    summed = scatter_sum(partials)
    hidden = (jax.nn.silu(summed[:, :proj_width]) * summed[:, proj_width:]).astype(jnp.bfloat16)
    hidden = gather_groups(hidden)
    return jnp.dot(hidden, w_down, preferred_element_type=jnp.float32).astype(jnp.bfloat16)


def backward_expert(row_block, grad_block, w_gate, w_up, w_down):
    proj_width = w_gate.shape[1]
    partials = jnp.concatenate(
        [
            jnp.dot(row_block, w_gate, preferred_element_type=jnp.float32),
            jnp.dot(row_block, w_up, preferred_element_type=jnp.float32),
        ],
        axis=1,
    ).astype(jnp.bfloat16)
    grad_part = contract_cols(grad_block, w_down).astype(jnp.bfloat16)
    summed = scatter_sum(jnp.concatenate([partials, grad_part], axis=1))
    gate_value = summed[:, :proj_width]
    up_value = summed[:, proj_width : 2 * proj_width]
    grad_hidden = summed[:, 2 * proj_width :]
    sigmoid_value = jax.nn.sigmoid(gate_value)
    grad_gate = (
        grad_hidden * up_value * sigmoid_value * (1.0 + gate_value * (1.0 - sigmoid_value))
    ).astype(jnp.bfloat16)
    grad_up = (grad_hidden * gate_value * sigmoid_value).astype(jnp.bfloat16)
    grads = gather_groups(jnp.concatenate([grad_gate, grad_up], axis=1))
    result = contract_cols(grads[:, :proj_width], w_gate) + contract_cols(
        grads[:, proj_width:], w_up
    )
    return result.astype(jnp.bfloat16)


def on_device(
    fwd_tokens,
    fwd_routes,
    fwd_gates,
    bwd_tokens,
    bwd_grads,
    bwd_routes,
    bwd_gates,
    gate_proj,
    up_proj,
    down_proj,
):
    expert_count = lax.axis_size("ep") // 4
    tokens_fwd = fwd_tokens[0]
    tok_count = tokens_fwd.shape[0]
    route_width = fwd_routes.shape[2]
    slot_cap = 3 * tok_count * route_width // (2 * expert_count)
    places_fwd = slot_places(fwd_routes[0], expert_count, slot_cap)
    places_bwd = slot_places(bwd_routes[0], expert_count, slot_cap)
    send_fwd = device_rows(spread_rows(places_fwd, tokens_fwd))
    send_rows = device_rows(spread_rows(places_bwd, bwd_tokens[0]))
    slot_gate = jnp.einsum("tkec,tk->ec", places_bwd, bwd_gates[0], precision=lax.Precision.HIGHEST)
    send_grads = device_rows(spread_rows(places_bwd, bwd_grads[0]) * slot_gate[:, None, :, None])
    slot_cap_fwd = send_fwd.shape[1]
    received = lax.all_to_all(
        jnp.concatenate([send_fwd, send_rows, send_grads], axis=1),
        "ep",
        split_axis=0,
        concat_axis=0,
        tiled=True,
    )
    recv_fwd = received[:, :slot_cap_fwd]
    recv_rows = received[:, slot_cap_fwd : 2 * slot_cap_fwd]
    recv_grads = received[:, 2 * slot_cap_fwd :]
    quarter_width = send_fwd.shape[2]
    w_gate = gate_proj[0, 0]
    w_up = up_proj[0, 0]
    w_down = down_proj[0, 0]
    out_fwd = forward_expert(recv_fwd.reshape(-1, quarter_width), w_gate, w_up, w_down).reshape(
        recv_fwd.shape
    )
    out_bwd = backward_expert(
        recv_rows.reshape(-1, quarter_width),
        recv_grads.reshape(-1, quarter_width),
        w_gate,
        w_up,
        w_down,
    ).reshape(recv_rows.shape)
    back = lax.all_to_all(
        jnp.concatenate([out_fwd, out_bwd], axis=1), "ep", split_axis=0, concat_axis=0, tiled=True
    )
    back_fwd = back[:, :slot_cap_fwd]
    back_bwd = back[:, slot_cap_fwd:]
    gathered = collect(places_fwd, back_fwd)
    mixture = (
        jnp.sum(gathered * fwd_gates[0][:, :, None, None], axis=1)
        .reshape(tok_count, -1)
        .astype(jnp.bfloat16)
    )
    grad_input = (
        jnp.sum(collect(places_bwd, back_bwd), axis=1).reshape(tok_count, -1).astype(jnp.bfloat16)
    )
    handed_forward = shifted(mixture[None], "pp", 1)
    handed_backward = shifted(grad_input[None], "pp", -1)
    return (handed_forward, handed_backward)


def solution(mesh):
    return jax.shard_map(
        on_device,
        mesh=mesh,
        in_specs=(
            P("pp", "ep", None),
            P("pp", "ep", None),
            P("pp", "ep", None),
            P("pp", "ep", None),
            P("pp", "ep", None),
            P("pp", "ep", None),
            P("pp", "ep", None),
            P("pp", "ep", None, None),
            P("pp", "ep", None, None),
            P("pp", "ep", None, None),
        ),
        out_specs=(P("pp", "ep", None), P("pp", "ep", None)),
        check_vma=False,
    )
```

```python
import functools

import jax
import jax.numpy as jnp
from jax import lax
from jax.sharding import PartitionSpec as P
from jax.experimental import pallas as pl
from jax.experimental.pallas import tpu as pltpu


def partner(block, axis, distance):
    count = lax.axis_size(axis)
    route = []
    for low in range(count):
        high = low | 1 << distance
        if high != low and high < count:
            route += [(low, high), (high, low)]
    return lax.ppermute(block, axis, route)


def shifted(shard, axis, by):
    count = lax.axis_size(axis)
    pairs = [(i, i + by) for i in range(count) if 0 <= i + by < count]
    return lax.ppermute(shard, axis, pairs)


def slot_places(routes, expert_count, slot_cap):
    tok_count = routes.shape[0]
    route_width = routes.shape[1]
    flat_routes = routes.reshape(-1)
    onehot = (flat_routes[:, None] == jnp.arange(expert_count, dtype=jnp.int32)[None, :]).astype(
        jnp.int32
    )
    before = jnp.cumsum(onehot, axis=0) - onehot
    position = jnp.sum(before * onehot, axis=1)
    slot_match = (position[:, None] == jnp.arange(slot_cap, dtype=jnp.int32)[None, :]).astype(
        jnp.float32
    )
    placed = onehot.astype(jnp.float32)[:, :, None] * slot_match[:, None, :]
    return placed.reshape(tok_count, route_width, expert_count, slot_cap)


def spread_rows(places, values):
    tok_count = values.shape[0]
    quarter_width = values.shape[1] // 4
    return jnp.einsum(
        "tkec,thf->ehcf",
        places.astype(jnp.bfloat16),
        values.reshape(tok_count, 4, quarter_width),
        preferred_element_type=jnp.float32,
    )


def device_rows(placed):
    return placed.astype(jnp.bfloat16).reshape(
        4 * placed.shape[0], placed.shape[2], placed.shape[3]
    )


def collect(places, returned):
    expert_count = places.shape[2]
    shaped = returned.reshape(expert_count, 4, returned.shape[1], returned.shape[2])
    return jnp.einsum(
        "tkec,ehcf->tkhf", places.astype(jnp.bfloat16), shaped, preferred_element_type=jnp.float32
    )


def contract_cols(left, right):
    return lax.dot_general(
        left, right, (((1,), (1,)), ((), ())), preferred_element_type=jnp.float32
    )


def quarter_bits():
    quarter = lax.axis_index("ep") % 4
    return quarter // 2, quarter % 2


def pick(flag, when_set, when_clear):
    return jnp.where(flag == 1, when_set, when_clear)


def scatter_sum(partials):
    high, low = quarter_bits()
    grouped = partials.reshape(2, 2, partials.shape[0] // 4, partials.shape[1])
    keep_pair = pick(low, grouped[:, 1], grouped[:, 0])
    give_pair = pick(low, grouped[:, 0], grouped[:, 1])
    pair_sum = keep_pair.astype(jnp.float32) + partner(give_pair, "ep", 0).astype(jnp.float32)
    keep_group = pick(high, pair_sum[1], pair_sum[0])
    give_group = pick(high, pair_sum[0], pair_sum[1])
    return keep_group + partner(give_group, "ep", 1)


def gather_groups(block):
    high, low = quarter_bits()
    pair = jnp.stack([block, partner(block, "ep", 1)])
    held = jnp.stack([pair, partner(pair, "ep", 0)], axis=1)
    held = pick(high, held[::-1], held)
    held = pick(low, held[:, ::-1], held)
    return held.reshape(-1, block.shape[1])


def forward_expert(row_block, w_gate, w_up, w_down):
    proj_width = w_gate.shape[1]
    partials = jnp.concatenate(
        [
            jnp.dot(row_block, w_gate, preferred_element_type=jnp.float32),
            jnp.dot(row_block, w_up, preferred_element_type=jnp.float32),
        ],
        axis=1,
    ).astype(jnp.bfloat16)
    summed = scatter_sum(partials)
    hidden = (jax.nn.silu(summed[:, :proj_width]) * summed[:, proj_width:]).astype(jnp.bfloat16)
    hidden = gather_groups(hidden)
    return jnp.dot(hidden, w_down, preferred_element_type=jnp.float32).astype(jnp.bfloat16)


def backward_expert(row_block, grad_block, w_gate, w_up, w_down):
    proj_width = w_gate.shape[1]
    partials = jnp.concatenate(
        [
            jnp.dot(row_block, w_gate, preferred_element_type=jnp.float32),
            jnp.dot(row_block, w_up, preferred_element_type=jnp.float32),
        ],
        axis=1,
    ).astype(jnp.bfloat16)
    grad_part = contract_cols(grad_block, w_down).astype(jnp.bfloat16)
    summed = scatter_sum(jnp.concatenate([partials, grad_part], axis=1))
    gate_value = summed[:, :proj_width]
    up_value = summed[:, proj_width : 2 * proj_width]
    grad_hidden = summed[:, 2 * proj_width :]
    sigmoid_value = jax.nn.sigmoid(gate_value)
    grad_gate = (
        grad_hidden * up_value * sigmoid_value * (1.0 + gate_value * (1.0 - sigmoid_value))
    ).astype(jnp.bfloat16)
    grad_up = (grad_hidden * gate_value * sigmoid_value).astype(jnp.bfloat16)
    grads = gather_groups(jnp.concatenate([grad_gate, grad_up], axis=1))
    result = contract_cols(grads[:, :proj_width], w_gate) + contract_cols(
        grads[:, proj_width:], w_up
    )
    return result.astype(jnp.bfloat16)


def return_kernel(pp_count, ep_count, step, src_ref, dst_ref, send_sem, recv_sem):
    stage = lax.axis_index("pp")
    me = lax.axis_index("ep")
    sends = (stage + step >= 0) & (stage + step < pp_count)
    receives = (stage - step >= 0) & (stage - step < pp_count)
    mesh_ids = pl.DeviceIdType.MESH
    barrier = pltpu.get_barrier_semaphore()

    def each(body):
        @pl.loop(0, ep_count)
        def _(offset):
            body(lax.rem(me + 1 + offset, ep_count))

    def greet(target):
        each(lambda n: pl.semaphore_signal(barrier, 1, device_id=(target, n), device_id_type=mesh_ids))

    pl.when(sends)(lambda: greet(stage + step))
    pl.when(receives)(lambda: greet(stage - step))
    pl.when(sends & receives)(lambda: pl.semaphore_wait(barrier, 2 * ep_count))
    pl.when(sends != receives)(lambda: pl.semaphore_wait(barrier, ep_count))

    def copy(n, sender):
        return pltpu.make_async_remote_copy(
            src_ref=src_ref.at[n],
            dst_ref=dst_ref.at[sender],
            send_sem=send_sem.at[n],
            recv_sem=recv_sem.at[sender],
            device_id=(stage + step, n),
            device_id_type=mesh_ids,
        )

    pl.when(sends)(lambda: each(lambda n: copy(n, me).start()))
    pl.when(sends)(lambda: each(lambda n: copy(n, me).wait_send()))
    pl.when(receives)(lambda: each(lambda j: copy(me, j).wait_recv()))


def send_back(out_block, step, kernel_id):
    pp_count = lax.axis_size("pp")
    ep_count = lax.axis_size("ep")
    return pl.pallas_call(
        functools.partial(return_kernel, pp_count, ep_count, step),
        out_shape=jax.ShapeDtypeStruct(out_block.shape, out_block.dtype),
        in_specs=[pl.BlockSpec(memory_space=pl.ANY)],
        out_specs=pl.BlockSpec(memory_space=pl.ANY),
        scratch_shapes=[
            pltpu.SemaphoreType.DMA((ep_count,)),
            pltpu.SemaphoreType.DMA((ep_count,)),
        ],
        compiler_params=pltpu.CompilerParams(collective_id=kernel_id, has_side_effects=True),
    )(out_block)


def on_device(
    fwd_tokens,
    fwd_routes,
    fwd_gates,
    bwd_tokens,
    bwd_grads,
    bwd_routes,
    bwd_gates,
    gate_proj,
    up_proj,
    down_proj,
):
    expert_count = lax.axis_size("ep") // 4
    tokens_fwd = fwd_tokens[0]
    tok_count = tokens_fwd.shape[0]
    route_width = fwd_routes.shape[2]
    slot_cap = 3 * tok_count * route_width // (2 * expert_count)
    places_fwd = slot_places(fwd_routes[0], expert_count, slot_cap)
    places_bwd = slot_places(bwd_routes[0], expert_count, slot_cap)
    send_fwd = device_rows(spread_rows(places_fwd, tokens_fwd))
    send_rows = device_rows(spread_rows(places_bwd, bwd_tokens[0]))
    slot_gate = jnp.einsum("tkec,tk->ec", places_bwd, bwd_gates[0], precision=lax.Precision.HIGHEST)
    send_grads = device_rows(spread_rows(places_bwd, bwd_grads[0]) * slot_gate[:, None, :, None])
    recv_fwd = lax.all_to_all(send_fwd, "ep", split_axis=0, concat_axis=0, tiled=True)
    slot_cap_bwd = send_rows.shape[1]
    received = lax.all_to_all(
        jnp.concatenate([send_rows, send_grads], axis=1),
        "ep",
        split_axis=0,
        concat_axis=0,
        tiled=True,
    )
    recv_rows = received[:, :slot_cap_bwd]
    recv_grads = received[:, slot_cap_bwd:]
    quarter_width = send_fwd.shape[2]
    w_gate = gate_proj[0, 0]
    w_up = up_proj[0, 0]
    w_down = down_proj[0, 0]
    out_fwd = forward_expert(recv_fwd.reshape(-1, quarter_width), w_gate, w_up, w_down).reshape(
        recv_fwd.shape
    )
    out_bwd = backward_expert(
        recv_rows.reshape(-1, quarter_width),
        recv_grads.reshape(-1, quarter_width),
        w_gate,
        w_up,
        w_down,
    ).reshape(recv_rows.shape)
    back_fwd = send_back(out_fwd, 1, 0)
    back_bwd = send_back(out_bwd, -1, 1)
    stage = lax.axis_index("pp")
    pp_count = lax.axis_size("pp")
    routes_prev = shifted(fwd_routes, "pp", 1)
    gates_prev = shifted(fwd_gates, "pp", 1)
    routes_next = shifted(bwd_routes, "pp", -1)
    places_prev = slot_places(routes_prev[0], expert_count, slot_cap)
    places_next = slot_places(routes_next[0], expert_count, slot_cap)
    gathered = collect(places_prev, back_fwd)
    mixture = (
        jnp.sum(gathered * gates_prev[0][:, :, None, None], axis=1)
        .reshape(tok_count, -1)
        .astype(jnp.bfloat16)
    )
    grad_input = (
        jnp.sum(collect(places_next, back_bwd), axis=1).reshape(tok_count, -1).astype(jnp.bfloat16)
    )
    handed_forward = jnp.where(stage == 0, jnp.zeros_like(mixture), mixture)[None]
    handed_backward = jnp.where(stage == pp_count - 1, jnp.zeros_like(grad_input), grad_input)[None]
    return (handed_forward, handed_backward)


def solution(mesh):
    return jax.shard_map(
        on_device,
        mesh=mesh,
        in_specs=(
            P("pp", "ep", None),
            P("pp", "ep", None),
            P("pp", "ep", None),
            P("pp", "ep", None),
            P("pp", "ep", None),
            P("pp", "ep", None),
            P("pp", "ep", None),
            P("pp", "ep", None, None),
            P("pp", "ep", None, None),
            P("pp", "ep", None, None),
        ),
        out_specs=(P("pp", "ep", None), P("pp", "ep", None)),
        check_vma=False,
    )
```

```python
import functools

import jax
import jax.numpy as jnp
from jax import lax
from jax.sharding import PartitionSpec as P
from jax.experimental import pallas as pl
from jax.experimental.pallas import tpu as pltpu


def partner(block, axis, distance):
    count = lax.axis_size(axis)
    route = []
    for low in range(count):
        high = low | 1 << distance
        if high != low and high < count:
            route += [(low, high), (high, low)]
    return lax.ppermute(block, axis, route)


def shifted(shard, axis, by):
    count = lax.axis_size(axis)
    pairs = [(i, i + by) for i in range(count) if 0 <= i + by < count]
    return lax.ppermute(shard, axis, pairs)


def slot_places(routes, expert_count, slot_cap):
    tok_count = routes.shape[0]
    route_width = routes.shape[1]
    flat_routes = routes.reshape(-1)
    onehot = (flat_routes[:, None] == jnp.arange(expert_count, dtype=jnp.int32)[None, :]).astype(
        jnp.int32
    )
    before = jnp.cumsum(onehot, axis=0) - onehot
    position = jnp.sum(before * onehot, axis=1)
    slot_match = (position[:, None] == jnp.arange(slot_cap, dtype=jnp.int32)[None, :]).astype(
        jnp.float32
    )
    placed = onehot.astype(jnp.float32)[:, :, None] * slot_match[:, None, :]
    return placed.reshape(tok_count, route_width, expert_count, slot_cap)


def spread_rows(places, values):
    tok_count = values.shape[0]
    quarter_width = values.shape[1] // 4
    return jnp.einsum(
        "tkec,thf->ehcf",
        places.astype(jnp.bfloat16),
        values.reshape(tok_count, 4, quarter_width),
        preferred_element_type=jnp.float32,
    )


def device_rows(placed):
    return placed.astype(jnp.bfloat16).reshape(
        4 * placed.shape[0], placed.shape[2], placed.shape[3]
    )


def collect(places, returned):
    expert_count = places.shape[2]
    shaped = returned.reshape(expert_count, 4, returned.shape[1], returned.shape[2])
    return jnp.einsum(
        "tkec,ehcf->tkhf", places.astype(jnp.bfloat16), shaped, preferred_element_type=jnp.float32
    )


def contract_cols(left, right):
    return lax.dot_general(
        left, right, (((1,), (1,)), ((), ())), preferred_element_type=jnp.float32
    )


def quarter_bits():
    quarter = lax.axis_index("ep") % 4
    return quarter // 2, quarter % 2


def pick(flag, when_set, when_clear):
    return jnp.where(flag == 1, when_set, when_clear)


def scatter_sum(partials):
    high, low = quarter_bits()
    grouped = partials.reshape(2, 2, partials.shape[0] // 4, partials.shape[1])
    keep_half = pick(high, grouped[1], grouped[0])
    give_half = pick(high, grouped[0], grouped[1])
    pair_sum = keep_half.astype(jnp.float32) + partner(give_half, "ep", 1).astype(jnp.float32)
    keep_group = pick(low, pair_sum[1], pair_sum[0])
    give_group = pick(low, pair_sum[0], pair_sum[1])
    return keep_group + partner(give_group, "ep", 0)


def gather_groups(block):
    high, low = quarter_bits()
    pair = jnp.stack([block, partner(block, "ep", 1)])
    held = jnp.stack([pair, partner(pair, "ep", 0)], axis=1)
    held = pick(high, held[::-1], held)
    held = pick(low, held[:, ::-1], held)
    return held.reshape(-1, block.shape[1])


def forward_expert(row_block, w_gate, w_up, w_down):
    proj_width = w_gate.shape[1]
    partials = jnp.concatenate(
        [
            jnp.dot(row_block, w_gate, preferred_element_type=jnp.float32),
            jnp.dot(row_block, w_up, preferred_element_type=jnp.float32),
        ],
        axis=1,
    ).astype(jnp.bfloat16)
    summed = scatter_sum(partials)
    hidden = (jax.nn.silu(summed[:, :proj_width]) * summed[:, proj_width:]).astype(jnp.bfloat16)
    hidden = gather_groups(hidden)
    return jnp.dot(hidden, w_down, preferred_element_type=jnp.float32).astype(jnp.bfloat16)


def backward_expert(row_block, grad_block, w_gate, w_up, w_down):
    proj_width = w_gate.shape[1]
    partials = jnp.concatenate(
        [
            jnp.dot(row_block, w_gate, preferred_element_type=jnp.float32),
            jnp.dot(row_block, w_up, preferred_element_type=jnp.float32),
        ],
        axis=1,
    ).astype(jnp.bfloat16)
    grad_part = contract_cols(grad_block, w_down).astype(jnp.bfloat16)
    summed = scatter_sum(jnp.concatenate([partials, grad_part], axis=1))
    gate_value = summed[:, :proj_width]
    up_value = summed[:, proj_width : 2 * proj_width]
    grad_hidden = summed[:, 2 * proj_width :]
    sigmoid_value = jax.nn.sigmoid(gate_value)
    grad_gate = (
        grad_hidden * up_value * sigmoid_value * (1.0 + gate_value * (1.0 - sigmoid_value))
    ).astype(jnp.bfloat16)
    grad_up = (grad_hidden * gate_value * sigmoid_value).astype(jnp.bfloat16)
    grads = gather_groups(jnp.concatenate([grad_gate, grad_up], axis=1))
    result = contract_cols(grads[:, :proj_width], w_gate) + contract_cols(
        grads[:, proj_width:], w_up
    )
    return result.astype(jnp.bfloat16)


def return_kernel(pp_count, ep_count, fwd_ref, bwd_ref, fwd_out, bwd_out, send_sem, recv_sem):
    stage = lax.axis_index("pp")
    me = lax.axis_index("ep")
    has_next = stage < pp_count - 1
    has_prev = stage > 0
    mesh_ids = pl.DeviceIdType.MESH
    barrier = pltpu.get_barrier_semaphore()

    def greet(target):
        @pl.loop(0, ep_count)
        def _(n):
            pl.semaphore_signal(barrier, 1, device_id=(target, n), device_id_type=mesh_ids)

    pl.when(has_next)(lambda: greet(stage + 1))
    pl.when(has_prev)(lambda: greet(stage - 1))
    pl.when(has_next & has_prev)(lambda: pl.semaphore_wait(barrier, 2 * ep_count))
    pl.when(jnp.logical_not(has_next & has_prev))(lambda: pl.semaphore_wait(barrier, ep_count))

    def fwd_copy(n, sender):
        return pltpu.make_async_remote_copy(
            src_ref=fwd_ref.at[n],
            dst_ref=fwd_out.at[sender],
            send_sem=send_sem.at[0, n],
            recv_sem=recv_sem.at[0, sender],
            device_id=(stage + 1, n),
            device_id_type=mesh_ids,
        )

    def bwd_copy(n, sender):
        return pltpu.make_async_remote_copy(
            src_ref=bwd_ref.at[n],
            dst_ref=bwd_out.at[sender],
            send_sem=send_sem.at[1, n],
            recv_sem=recv_sem.at[1, sender],
            device_id=(stage - 1, n),
            device_id_type=mesh_ids,
        )

    def each(body):
        @pl.loop(0, ep_count)
        def _(step):
            body(lax.rem(me + 1 + step, ep_count))

    pl.when(has_next)(lambda: each(lambda n: fwd_copy(n, me).start()))
    pl.when(has_prev)(lambda: each(lambda n: bwd_copy(n, me).start()))
    pl.when(has_next)(lambda: each(lambda n: fwd_copy(n, me).wait_send()))
    pl.when(has_prev)(lambda: each(lambda n: bwd_copy(n, me).wait_send()))
    pl.when(has_prev)(lambda: each(lambda j: fwd_copy(me, j).wait_recv()))
    pl.when(has_next)(lambda: each(lambda j: bwd_copy(me, j).wait_recv()))


def send_back(out_fwd, out_bwd):
    pp_count = lax.axis_size("pp")
    ep_count = lax.axis_size("ep")
    chunk = jax.ShapeDtypeStruct(out_fwd.shape, out_fwd.dtype)
    return pl.pallas_call(
        functools.partial(return_kernel, pp_count, ep_count),
        out_shape=(chunk, chunk),
        in_specs=[pl.BlockSpec(memory_space=pl.ANY)] * 2,
        out_specs=(pl.BlockSpec(memory_space=pl.ANY), pl.BlockSpec(memory_space=pl.ANY)),
        scratch_shapes=[
            pltpu.SemaphoreType.DMA((2, ep_count)),
            pltpu.SemaphoreType.DMA((2, ep_count)),
        ],
        compiler_params=pltpu.CompilerParams(collective_id=0, has_side_effects=True),
    )(out_fwd, out_bwd)


def on_device(
    fwd_tokens,
    fwd_routes,
    fwd_gates,
    bwd_tokens,
    bwd_grads,
    bwd_routes,
    bwd_gates,
    gate_proj,
    up_proj,
    down_proj,
):
    expert_count = lax.axis_size("ep") // 4
    tokens_fwd = fwd_tokens[0]
    tok_count = tokens_fwd.shape[0]
    route_width = fwd_routes.shape[2]
    slot_cap = 3 * tok_count * route_width // (2 * expert_count)
    places_fwd = slot_places(fwd_routes[0], expert_count, slot_cap)
    places_bwd = slot_places(bwd_routes[0], expert_count, slot_cap)
    send_fwd = device_rows(spread_rows(places_fwd, tokens_fwd))
    send_rows = device_rows(spread_rows(places_bwd, bwd_tokens[0]))
    slot_gate = jnp.einsum("tkec,tk->ec", places_bwd, bwd_gates[0], precision=lax.Precision.HIGHEST)
    send_grads = device_rows(spread_rows(places_bwd, bwd_grads[0]) * slot_gate[:, None, :, None])
    slot_cap_fwd = send_fwd.shape[1]
    received = lax.all_to_all(
        jnp.concatenate([send_fwd, send_rows, send_grads], axis=1),
        "ep",
        split_axis=0,
        concat_axis=0,
        tiled=True,
    )
    recv_fwd = received[:, :slot_cap_fwd]
    recv_rows = received[:, slot_cap_fwd : 2 * slot_cap_fwd]
    recv_grads = received[:, 2 * slot_cap_fwd :]
    quarter_width = send_fwd.shape[2]
    w_gate = gate_proj[0, 0]
    w_up = up_proj[0, 0]
    w_down = down_proj[0, 0]
    out_fwd = forward_expert(recv_fwd.reshape(-1, quarter_width), w_gate, w_up, w_down).reshape(
        recv_fwd.shape
    )
    out_bwd = backward_expert(
        recv_rows.reshape(-1, quarter_width),
        recv_grads.reshape(-1, quarter_width),
        w_gate,
        w_up,
        w_down,
    ).reshape(recv_rows.shape)
    back_fwd, back_bwd = send_back(out_fwd, out_bwd)
    stage = lax.axis_index("pp")
    pp_count = lax.axis_size("pp")
    routes_prev = shifted(fwd_routes, "pp", 1)
    gates_prev = shifted(fwd_gates, "pp", 1)
    routes_next = shifted(bwd_routes, "pp", -1)
    places_prev = slot_places(routes_prev[0], expert_count, slot_cap)
    places_next = slot_places(routes_next[0], expert_count, slot_cap)
    gathered = collect(places_prev, back_fwd)
    mixture = (
        jnp.sum(gathered * gates_prev[0][:, :, None, None], axis=1)
        .reshape(tok_count, -1)
        .astype(jnp.bfloat16)
    )
    grad_input = (
        jnp.sum(collect(places_next, back_bwd), axis=1).reshape(tok_count, -1).astype(jnp.bfloat16)
    )
    handed_forward = jnp.where(stage == 0, jnp.zeros_like(mixture), mixture)[None]
    handed_backward = jnp.where(stage == pp_count - 1, jnp.zeros_like(grad_input), grad_input)[None]
    return (handed_forward, handed_backward)


def solution(mesh):
    return jax.shard_map(
        on_device,
        mesh=mesh,
        in_specs=(
            P("pp", "ep", None),
            P("pp", "ep", None),
            P("pp", "ep", None),
            P("pp", "ep", None),
            P("pp", "ep", None),
            P("pp", "ep", None),
            P("pp", "ep", None),
            P("pp", "ep", None, None),
            P("pp", "ep", None, None),
            P("pp", "ep", None, None),
        ),
        out_specs=(P("pp", "ep", None), P("pp", "ep", None)),
        check_vma=False,
    )
```

```python
import functools

import jax
import jax.numpy as jnp
from jax import lax
from jax.sharding import PartitionSpec as P
from jax.experimental import pallas as pl
from jax.experimental.pallas import tpu as pltpu


def partner(block, axis, distance):
    count = lax.axis_size(axis)
    route = []
    for low in range(count):
        high = low | 1 << distance
        if high != low and high < count:
            route += [(low, high), (high, low)]
    return lax.ppermute(block, axis, route)


def shifted(shard, axis, by):
    count = lax.axis_size(axis)
    pairs = [(i, i + by) for i in range(count) if 0 <= i + by < count]
    return lax.ppermute(shard, axis, pairs)


def slot_places(routes, expert_count, slot_cap):
    tok_count = routes.shape[0]
    route_width = routes.shape[1]
    flat_routes = routes.reshape(-1)
    onehot = (flat_routes[:, None] == jnp.arange(expert_count, dtype=jnp.int32)[None, :]).astype(
        jnp.int32
    )
    before = jnp.cumsum(onehot, axis=0) - onehot
    position = jnp.sum(before * onehot, axis=1)
    slot_match = (position[:, None] == jnp.arange(slot_cap, dtype=jnp.int32)[None, :]).astype(
        jnp.float32
    )
    placed = onehot.astype(jnp.float32)[:, :, None] * slot_match[:, None, :]
    return placed.reshape(tok_count, route_width, expert_count, slot_cap)


def spread_rows(places, values):
    tok_count = values.shape[0]
    quarter_width = values.shape[1] // 4
    return jnp.einsum(
        "tkec,thf->ehcf",
        places.astype(jnp.bfloat16),
        values.reshape(tok_count, 4, quarter_width),
        preferred_element_type=jnp.float32,
    )


def device_rows(placed):
    return placed.astype(jnp.bfloat16).reshape(
        4 * placed.shape[0], placed.shape[2], placed.shape[3]
    )


def collect(places, returned):
    expert_count = places.shape[2]
    shaped = returned.reshape(expert_count, 4, returned.shape[1], returned.shape[2])
    return jnp.einsum(
        "tkec,ehcf->tkhf", places.astype(jnp.bfloat16), shaped, preferred_element_type=jnp.float32
    )


def contract_cols(left, right):
    return lax.dot_general(
        left, right, (((1,), (1,)), ((), ())), preferred_element_type=jnp.float32
    )


def quarter_bits():
    quarter = lax.axis_index("ep") % 4
    return quarter // 2, quarter % 2


def pick(flag, when_set, when_clear):
    return jax.tree.map(lambda a, b: jnp.where(flag == 1, a, b), when_set, when_clear)


def scatter_sum(partials):
    high, low = quarter_bits()
    grouped = [p.reshape(2, 2, p.shape[0] // 4, p.shape[1]) for p in partials]
    keep_pair = pick(low, [g[:, 1] for g in grouped], [g[:, 0] for g in grouped])
    give_pair = pick(low, [g[:, 0] for g in grouped], [g[:, 1] for g in grouped])
    pair_sum = jax.tree.map(
        lambda a, b: a.astype(jnp.float32) + b.astype(jnp.float32),
        keep_pair,
        partner(give_pair, "ep", 0),
    )
    keep_group = pick(high, [p[1] for p in pair_sum], [p[0] for p in pair_sum])
    give_group = pick(high, [p[0] for p in pair_sum], [p[1] for p in pair_sum])
    return jax.tree.map(jnp.add, keep_group, partner(give_group, "ep", 1))


def gather_groups(blocks):
    high, low = quarter_bits()
    pair = jax.tree.map(lambda b, o: jnp.stack([b, o]), blocks, partner(blocks, "ep", 1))
    held = jax.tree.map(lambda b, o: jnp.stack([b, o], axis=1), pair, partner(pair, "ep", 0))
    held = pick(high, [h[::-1] for h in held], held)
    held = pick(low, [h[:, ::-1] for h in held], held)
    return [h.reshape(-1, h.shape[-1]) for h in held]


def forward_expert(row_block, w_gate, w_up, w_down):
    gate_part = jnp.dot(row_block, w_gate, preferred_element_type=jnp.float32).astype(jnp.bfloat16)
    up_part = jnp.dot(row_block, w_up, preferred_element_type=jnp.float32).astype(jnp.bfloat16)
    gate_value, up_value = scatter_sum([gate_part, up_part])
    hidden = (jax.nn.silu(gate_value) * up_value).astype(jnp.bfloat16)
    (hidden,) = gather_groups([hidden])
    return jnp.dot(hidden, w_down, preferred_element_type=jnp.float32).astype(jnp.bfloat16)


def backward_expert(row_block, grad_block, w_gate, w_up, w_down):
    gate_part = jnp.dot(row_block, w_gate, preferred_element_type=jnp.float32).astype(jnp.bfloat16)
    up_part = jnp.dot(row_block, w_up, preferred_element_type=jnp.float32).astype(jnp.bfloat16)
    grad_part = contract_cols(grad_block, w_down).astype(jnp.bfloat16)
    gate_value, up_value, grad_hidden = scatter_sum([gate_part, up_part, grad_part])
    sigmoid_value = jax.nn.sigmoid(gate_value)
    grad_gate = (
        grad_hidden * up_value * sigmoid_value * (1.0 + gate_value * (1.0 - sigmoid_value))
    ).astype(jnp.bfloat16)
    grad_up = (grad_hidden * gate_value * sigmoid_value).astype(jnp.bfloat16)
    grad_gate, grad_up = gather_groups([grad_gate, grad_up])
    result = contract_cols(grad_gate, w_gate) + contract_cols(grad_up, w_up)
    return result.astype(jnp.bfloat16)


def return_kernel(pp_count, ep_count, fwd_ref, bwd_ref, fwd_out, bwd_out, send_sem, recv_sem):
    stage = lax.axis_index("pp")
    me = lax.axis_index("ep")
    has_next = stage < pp_count - 1
    has_prev = stage > 0
    mesh_ids = pl.DeviceIdType.MESH
    barrier = pltpu.get_barrier_semaphore()

    def greet(target):
        @pl.loop(0, ep_count)
        def _(n):
            pl.semaphore_signal(barrier, 1, device_id=(target, n), device_id_type=mesh_ids)

    pl.when(has_next)(lambda: greet(stage + 1))
    pl.when(has_prev)(lambda: greet(stage - 1))
    pl.when(has_next & has_prev)(lambda: pl.semaphore_wait(barrier, 2 * ep_count))
    pl.when(jnp.logical_not(has_next & has_prev))(lambda: pl.semaphore_wait(barrier, ep_count))

    half = fwd_ref.shape[2] // 2

    def fwd_copy(n, sender, part):
        cols = pl.ds(part * half, half)
        return pltpu.make_async_remote_copy(
            src_ref=fwd_ref.at[n, :, cols],
            dst_ref=fwd_out.at[sender, :, cols],
            send_sem=send_sem.at[0, part, n],
            recv_sem=recv_sem.at[0, part, sender],
            device_id=(stage + 1, n),
            device_id_type=mesh_ids,
        )

    def bwd_copy(n, sender, part):
        cols = pl.ds(part * half, half)
        return pltpu.make_async_remote_copy(
            src_ref=bwd_ref.at[n, :, cols],
            dst_ref=bwd_out.at[sender, :, cols],
            send_sem=send_sem.at[1, part, n],
            recv_sem=recv_sem.at[1, part, sender],
            device_id=(stage - 1, n),
            device_id_type=mesh_ids,
        )

    def each(body):
        @pl.loop(0, ep_count)
        def _(step):
            body(lax.rem(me + 1 + step, ep_count))

    def start_both(n):
        for part in range(2):
            pl.when(has_next)(lambda: fwd_copy(n, me, part).start())
            pl.when(has_prev)(lambda: bwd_copy(n, me, part).start())

    def for_parts(body):
        return lambda n: [body(n, part) for part in range(2)]

    each(start_both)
    pl.when(has_next)(lambda: each(for_parts(lambda n, part: fwd_copy(n, me, part).wait_send())))
    pl.when(has_prev)(lambda: each(for_parts(lambda n, part: bwd_copy(n, me, part).wait_send())))
    pl.when(has_prev)(lambda: each(for_parts(lambda j, part: fwd_copy(me, j, part).wait_recv())))
    pl.when(has_next)(lambda: each(for_parts(lambda j, part: bwd_copy(me, j, part).wait_recv())))


def send_back(out_fwd, out_bwd):
    pp_count = lax.axis_size("pp")
    ep_count = lax.axis_size("ep")
    chunk = jax.ShapeDtypeStruct(out_fwd.shape, out_fwd.dtype)
    return pl.pallas_call(
        functools.partial(return_kernel, pp_count, ep_count),
        out_shape=(chunk, chunk),
        in_specs=[pl.BlockSpec(memory_space=pl.ANY)] * 2,
        out_specs=(pl.BlockSpec(memory_space=pl.ANY), pl.BlockSpec(memory_space=pl.ANY)),
        scratch_shapes=[
            pltpu.SemaphoreType.DMA((2, 2, ep_count)),
            pltpu.SemaphoreType.DMA((2, 2, ep_count)),
        ],
        compiler_params=pltpu.CompilerParams(collective_id=0, has_side_effects=True),
    )(out_fwd, out_bwd)


def on_device(
    fwd_tokens,
    fwd_routes,
    fwd_gates,
    bwd_tokens,
    bwd_grads,
    bwd_routes,
    bwd_gates,
    gate_proj,
    up_proj,
    down_proj,
):
    expert_count = lax.axis_size("ep") // 4
    tokens_fwd = fwd_tokens[0]
    tok_count = tokens_fwd.shape[0]
    route_width = fwd_routes.shape[2]
    slot_cap = 3 * tok_count * route_width // (2 * expert_count)
    places_fwd = slot_places(fwd_routes[0], expert_count, slot_cap)
    places_bwd = slot_places(bwd_routes[0], expert_count, slot_cap)
    send_fwd = device_rows(spread_rows(places_fwd, tokens_fwd))
    send_rows = device_rows(spread_rows(places_bwd, bwd_tokens[0]))
    slot_gate = jnp.einsum("tkec,tk->ec", places_bwd, bwd_gates[0], precision=lax.Precision.HIGHEST)
    send_grads = device_rows(spread_rows(places_bwd, bwd_grads[0]) * slot_gate[:, None, :, None])
    slot_cap_fwd = send_fwd.shape[1]
    received = lax.all_to_all(
        jnp.concatenate([send_fwd, send_rows, send_grads], axis=1),
        "ep",
        split_axis=0,
        concat_axis=0,
        tiled=True,
    )
    recv_fwd = received[:, :slot_cap_fwd]
    recv_rows = received[:, slot_cap_fwd : 2 * slot_cap_fwd]
    recv_grads = received[:, 2 * slot_cap_fwd :]
    quarter_width = send_fwd.shape[2]
    w_gate = gate_proj[0, 0]
    w_up = up_proj[0, 0]
    w_down = down_proj[0, 0]
    out_fwd = forward_expert(recv_fwd.reshape(-1, quarter_width), w_gate, w_up, w_down).reshape(
        recv_fwd.shape
    )
    out_bwd = backward_expert(
        recv_rows.reshape(-1, quarter_width),
        recv_grads.reshape(-1, quarter_width),
        w_gate,
        w_up,
        w_down,
    ).reshape(recv_rows.shape)
    back_fwd, back_bwd = send_back(out_fwd, out_bwd)
    stage = lax.axis_index("pp")
    pp_count = lax.axis_size("pp")
    routes_prev = shifted(fwd_routes, "pp", 1)
    gates_prev = shifted(fwd_gates, "pp", 1)
    routes_next = shifted(bwd_routes, "pp", -1)
    places_prev = slot_places(routes_prev[0], expert_count, slot_cap)
    places_next = slot_places(routes_next[0], expert_count, slot_cap)
    gathered = collect(places_prev, back_fwd)
    mixture = (
        jnp.sum(gathered * gates_prev[0][:, :, None, None], axis=1)
        .reshape(tok_count, -1)
        .astype(jnp.bfloat16)
    )
    grad_input = (
        jnp.sum(collect(places_next, back_bwd), axis=1).reshape(tok_count, -1).astype(jnp.bfloat16)
    )
    handed_forward = jnp.where(stage == 0, jnp.zeros_like(mixture), mixture)[None]
    handed_backward = jnp.where(stage == pp_count - 1, jnp.zeros_like(grad_input), grad_input)[None]
    return (handed_forward, handed_backward)


def solution(mesh):
    return jax.shard_map(
        on_device,
        mesh=mesh,
        in_specs=(
            P("pp", "ep", None),
            P("pp", "ep", None),
            P("pp", "ep", None),
            P("pp", "ep", None),
            P("pp", "ep", None),
            P("pp", "ep", None),
            P("pp", "ep", None),
            P("pp", "ep", None, None),
            P("pp", "ep", None, None),
            P("pp", "ep", None, None),
        ),
        out_specs=(P("pp", "ep", None), P("pp", "ep", None)),
        check_vma=False,
    )
```

```python
import functools

import jax
import jax.numpy as jnp
from jax import lax
from jax.sharding import PartitionSpec as P
from jax.experimental import pallas as pl
from jax.experimental.pallas import tpu as pltpu


def partner(block, axis, distance):
    count = lax.axis_size(axis)
    route = []
    for low in range(count):
        high = low | 1 << distance
        if high != low and high < count:
            route += [(low, high), (high, low)]
    return lax.ppermute(block, axis, route)


def shifted(shard, axis, by):
    count = lax.axis_size(axis)
    pairs = [(i, i + by) for i in range(count) if 0 <= i + by < count]
    return lax.ppermute(shard, axis, pairs)


def slot_places(routes, expert_count, slot_cap):
    tok_count = routes.shape[0]
    route_width = routes.shape[1]
    flat_routes = routes.reshape(-1)
    onehot = (flat_routes[:, None] == jnp.arange(expert_count, dtype=jnp.int32)[None, :]).astype(
        jnp.int32
    )
    before = jnp.cumsum(onehot, axis=0) - onehot
    position = jnp.sum(before * onehot, axis=1)
    slot_match = (position[:, None] == jnp.arange(slot_cap, dtype=jnp.int32)[None, :]).astype(
        jnp.float32
    )
    placed = onehot.astype(jnp.float32)[:, :, None] * slot_match[:, None, :]
    return placed.reshape(tok_count, route_width, expert_count, slot_cap)


def spread_rows(places, values):
    tok_count = values.shape[0]
    quarter_width = values.shape[1] // 4
    return jnp.einsum(
        "tkec,thf->ehcf",
        places.astype(jnp.bfloat16),
        values.reshape(tok_count, 4, quarter_width),
        preferred_element_type=jnp.float32,
    )


def device_rows(placed):
    return placed.astype(jnp.bfloat16).reshape(
        4 * placed.shape[0], placed.shape[2], placed.shape[3]
    )


def collect(places, returned):
    expert_count = places.shape[2]
    shaped = returned.reshape(expert_count, 4, returned.shape[1], returned.shape[2])
    return jnp.einsum(
        "tkec,ehcf->tkhf", places.astype(jnp.bfloat16), shaped, preferred_element_type=jnp.float32
    )


def contract_cols(left, right):
    return lax.dot_general(
        left, right, (((1,), (1,)), ((), ())), preferred_element_type=jnp.float32
    )


def quarter_bits():
    quarter = lax.axis_index("ep") % 4
    return quarter // 2, quarter % 2


def pick(flag, when_set, when_clear):
    return jax.tree.map(lambda a, b: jnp.where(flag == 1, a, b), when_set, when_clear)


def scatter_sum(partials):
    high, low = quarter_bits()
    grouped = [p.reshape(2, 2, p.shape[0] // 4, p.shape[1]) for p in partials]
    keep_pair = pick(low, [g[:, 1] for g in grouped], [g[:, 0] for g in grouped])
    give_pair = pick(low, [g[:, 0] for g in grouped], [g[:, 1] for g in grouped])
    pair_sum = jax.tree.map(
        lambda a, b: a.astype(jnp.float32) + b.astype(jnp.float32),
        keep_pair,
        partner(give_pair, "ep", 0),
    )
    keep_group = pick(high, [p[1] for p in pair_sum], [p[0] for p in pair_sum])
    give_group = pick(high, [p[0] for p in pair_sum], [p[1] for p in pair_sum])
    return jax.tree.map(jnp.add, keep_group, partner(give_group, "ep", 1))


def gather_groups(blocks):
    high, low = quarter_bits()
    pair = jax.tree.map(lambda b, o: jnp.stack([b, o]), blocks, partner(blocks, "ep", 1))
    held = jax.tree.map(lambda b, o: jnp.stack([b, o], axis=1), pair, partner(pair, "ep", 0))
    held = pick(high, [h[::-1] for h in held], held)
    held = pick(low, [h[:, ::-1] for h in held], held)
    return [h.reshape(-1, h.shape[-1]) for h in held]


def forward_expert(row_block, w_gate, w_up, w_down):
    gate_part = jnp.dot(row_block, w_gate, preferred_element_type=jnp.float32).astype(jnp.bfloat16)
    up_part = jnp.dot(row_block, w_up, preferred_element_type=jnp.float32).astype(jnp.bfloat16)
    gate_value, up_value = scatter_sum([gate_part, up_part])
    hidden = (jax.nn.silu(gate_value) * up_value).astype(jnp.bfloat16)
    (hidden,) = gather_groups([hidden])
    return jnp.dot(hidden, w_down, preferred_element_type=jnp.float32).astype(jnp.bfloat16)


def backward_expert(row_block, grad_block, w_gate, w_up, w_down):
    gate_part = jnp.dot(row_block, w_gate, preferred_element_type=jnp.float32).astype(jnp.bfloat16)
    up_part = jnp.dot(row_block, w_up, preferred_element_type=jnp.float32).astype(jnp.bfloat16)
    grad_part = contract_cols(grad_block, w_down).astype(jnp.bfloat16)
    gate_value, up_value, grad_hidden = scatter_sum([gate_part, up_part, grad_part])
    sigmoid_value = jax.nn.sigmoid(gate_value)
    grad_gate = (
        grad_hidden * up_value * sigmoid_value * (1.0 + gate_value * (1.0 - sigmoid_value))
    ).astype(jnp.bfloat16)
    grad_up = (grad_hidden * gate_value * sigmoid_value).astype(jnp.bfloat16)
    grad_gate, grad_up = gather_groups([grad_gate, grad_up])
    result = contract_cols(grad_gate, w_gate) + contract_cols(grad_up, w_up)
    return result.astype(jnp.bfloat16)


def return_kernel(pp_count, ep_count, fwd_ref, bwd_ref, fwd_out, bwd_out, send_sem, recv_sem):
    stage = lax.axis_index("pp")
    me = lax.axis_index("ep")
    has_next = stage < pp_count - 1
    has_prev = stage > 0
    mesh_ids = pl.DeviceIdType.MESH
    barrier = pltpu.get_barrier_semaphore()

    def greet(target):
        @pl.loop(0, ep_count)
        def _(n):
            pl.semaphore_signal(barrier, 1, device_id=(target, n), device_id_type=mesh_ids)

    pl.when(has_next)(lambda: greet(stage + 1))
    pl.when(has_prev)(lambda: greet(stage - 1))
    pl.when(has_next & has_prev)(lambda: pl.semaphore_wait(barrier, 2 * ep_count))
    pl.when(jnp.logical_not(has_next & has_prev))(lambda: pl.semaphore_wait(barrier, ep_count))

    def fwd_copy(n, sender):
        return pltpu.make_async_remote_copy(
            src_ref=fwd_ref.at[n],
            dst_ref=fwd_out.at[sender],
            send_sem=send_sem.at[0, n],
            recv_sem=recv_sem.at[0, sender],
            device_id=(stage + 1, n),
            device_id_type=mesh_ids,
        )

    def bwd_copy(n, sender):
        return pltpu.make_async_remote_copy(
            src_ref=bwd_ref.at[n],
            dst_ref=bwd_out.at[sender],
            send_sem=send_sem.at[1, n],
            recv_sem=recv_sem.at[1, sender],
            device_id=(stage - 1, n),
            device_id_type=mesh_ids,
        )

    def each(body):
        @pl.loop(0, ep_count)
        def _(step):
            body(lax.rem(me + 1 + step, ep_count))

    def start_both(n):
        pl.when(has_next)(lambda: fwd_copy(n, me).start())
        pl.when(has_prev)(lambda: bwd_copy(n, me).start())

    each(start_both)
    pl.when(has_next)(lambda: each(lambda n: fwd_copy(n, me).wait_send()))
    pl.when(has_prev)(lambda: each(lambda n: bwd_copy(n, me).wait_send()))
    pl.when(has_prev)(lambda: each(lambda j: fwd_copy(me, j).wait_recv()))
    pl.when(has_next)(lambda: each(lambda j: bwd_copy(me, j).wait_recv()))


def send_back(out_fwd, out_bwd):
    pp_count = lax.axis_size("pp")
    ep_count = lax.axis_size("ep")
    chunk = jax.ShapeDtypeStruct(out_fwd.shape, out_fwd.dtype)
    return pl.pallas_call(
        functools.partial(return_kernel, pp_count, ep_count),
        out_shape=(chunk, chunk),
        in_specs=[pl.BlockSpec(memory_space=pl.ANY)] * 2,
        out_specs=(pl.BlockSpec(memory_space=pl.ANY), pl.BlockSpec(memory_space=pl.ANY)),
        scratch_shapes=[
            pltpu.SemaphoreType.DMA((2, ep_count)),
            pltpu.SemaphoreType.DMA((2, ep_count)),
        ],
        compiler_params=pltpu.CompilerParams(collective_id=0, has_side_effects=True),
    )(out_fwd, out_bwd)


def on_device(
    fwd_tokens,
    fwd_routes,
    fwd_gates,
    bwd_tokens,
    bwd_grads,
    bwd_routes,
    bwd_gates,
    gate_proj,
    up_proj,
    down_proj,
):
    expert_count = lax.axis_size("ep") // 4
    tokens_fwd = fwd_tokens[0]
    tok_count = tokens_fwd.shape[0]
    route_width = fwd_routes.shape[2]
    slot_cap = 3 * tok_count * route_width // (2 * expert_count)
    places_fwd = slot_places(fwd_routes[0], expert_count, slot_cap)
    places_bwd = slot_places(bwd_routes[0], expert_count, slot_cap)
    slot_gate = jnp.einsum("tkec,tk->ec", places_bwd, bwd_gates[0], precision=lax.Precision.HIGHEST)
    flat_fwd = jnp.sum(places_fwd, axis=1)
    flat_bwd = jnp.sum(places_bwd, axis=1)
    blank = jnp.zeros_like(flat_fwd)
    stream_places = jnp.concatenate(
        [
            jnp.stack([flat_fwd, blank, blank], axis=2),
            jnp.stack([blank, flat_bwd, blank], axis=2),
            jnp.stack([blank, blank, flat_bwd], axis=2),
        ],
        axis=0,
    ).astype(jnp.bfloat16)
    stream_rows = jnp.concatenate([tokens_fwd, bwd_tokens[0], bwd_grads[0]], axis=0)
    quarter_width = tokens_fwd.shape[1] // 4
    spread = jnp.einsum(
        "tesc,thf->ehscf",
        stream_places,
        stream_rows.reshape(stream_rows.shape[0], 4, quarter_width),
        preferred_element_type=jnp.float32,
    )
    ones = jnp.ones_like(slot_gate)
    stream_scale = jnp.stack([ones, ones, slot_gate], axis=1)[:, None, :, :, None]
    send_all = (spread * stream_scale).astype(jnp.bfloat16)
    slot_cap_fwd = slot_cap
    received = lax.all_to_all(
        send_all.reshape(4 * expert_count, 3 * slot_cap, quarter_width),
        "ep",
        split_axis=0,
        concat_axis=0,
        tiled=True,
    )
    recv_fwd = received[:, :slot_cap_fwd]
    recv_rows = received[:, slot_cap_fwd : 2 * slot_cap_fwd]
    recv_grads = received[:, 2 * slot_cap_fwd :]
    w_gate = gate_proj[0, 0]
    w_up = up_proj[0, 0]
    w_down = down_proj[0, 0]
    out_fwd = forward_expert(recv_fwd.reshape(-1, quarter_width), w_gate, w_up, w_down).reshape(
        recv_fwd.shape
    )
    out_bwd = backward_expert(
        recv_rows.reshape(-1, quarter_width),
        recv_grads.reshape(-1, quarter_width),
        w_gate,
        w_up,
        w_down,
    ).reshape(recv_rows.shape)
    back_fwd, back_bwd = send_back(out_fwd, out_bwd)
    stage = lax.axis_index("pp")
    pp_count = lax.axis_size("pp")
    routes_prev = shifted(fwd_routes, "pp", 1)
    gates_prev = shifted(fwd_gates, "pp", 1)
    routes_next = shifted(bwd_routes, "pp", -1)
    places_prev = slot_places(routes_prev[0], expert_count, slot_cap)
    places_next = slot_places(routes_next[0], expert_count, slot_cap)
    gathered = collect(places_prev, back_fwd)
    mixture = (
        jnp.sum(gathered * gates_prev[0][:, :, None, None], axis=1)
        .reshape(tok_count, -1)
        .astype(jnp.bfloat16)
    )
    grad_input = (
        jnp.sum(collect(places_next, back_bwd), axis=1).reshape(tok_count, -1).astype(jnp.bfloat16)
    )
    handed_forward = jnp.where(stage == 0, jnp.zeros_like(mixture), mixture)[None]
    handed_backward = jnp.where(stage == pp_count - 1, jnp.zeros_like(grad_input), grad_input)[None]
    return (handed_forward, handed_backward)


def solution(mesh):
    return jax.shard_map(
        on_device,
        mesh=mesh,
        in_specs=(
            P("pp", "ep", None),
            P("pp", "ep", None),
            P("pp", "ep", None),
            P("pp", "ep", None),
            P("pp", "ep", None),
            P("pp", "ep", None),
            P("pp", "ep", None),
            P("pp", "ep", None, None),
            P("pp", "ep", None, None),
            P("pp", "ep", None, None),
        ),
        out_specs=(P("pp", "ep", None), P("pp", "ep", None)),
        check_vma=False,
    )
```

```python
import functools

import jax
import jax.numpy as jnp
from jax import lax
from jax.sharding import PartitionSpec as P
from jax.experimental import pallas as pl
from jax.experimental.pallas import tpu as pltpu


def partner(block, axis, distance):
    count = lax.axis_size(axis)
    route = []
    for low in range(count):
        high = low | 1 << distance
        if high != low and high < count:
            route += [(low, high), (high, low)]
    return lax.ppermute(block, axis, route)


def shifted(shard, axis, by):
    count = lax.axis_size(axis)
    pairs = [(i, i + by) for i in range(count) if 0 <= i + by < count]
    return lax.ppermute(shard, axis, pairs)


def slot_places(routes, expert_count, slot_cap):
    tok_count = routes.shape[0]
    route_width = routes.shape[1]
    flat_routes = routes.reshape(-1)
    onehot = (flat_routes[:, None] == jnp.arange(expert_count, dtype=jnp.int32)[None, :]).astype(
        jnp.int32
    )
    before = jnp.cumsum(onehot, axis=0) - onehot
    position = jnp.sum(before * onehot, axis=1)
    slot_match = (position[:, None] == jnp.arange(slot_cap, dtype=jnp.int32)[None, :]).astype(
        jnp.float32
    )
    placed = onehot.astype(jnp.float32)[:, :, None] * slot_match[:, None, :]
    return placed.reshape(tok_count, route_width, expert_count, slot_cap)


def spread_rows(places, values):
    tok_count = values.shape[0]
    quarter_width = values.shape[1] // 4
    return jnp.einsum(
        "tkec,thf->ehcf",
        places.astype(jnp.bfloat16),
        values.reshape(tok_count, 4, quarter_width),
        preferred_element_type=jnp.float32,
    )


def device_rows(placed):
    return placed.astype(jnp.bfloat16).reshape(
        4 * placed.shape[0], placed.shape[2], placed.shape[3]
    )


def collect(places, returned):
    expert_count = places.shape[2]
    shaped = returned.reshape(expert_count, 4, returned.shape[1], returned.shape[2])
    return jnp.einsum(
        "tkec,ehcf->tkhf", places.astype(jnp.bfloat16), shaped, preferred_element_type=jnp.float32
    )


def contract_cols(left, right):
    return lax.dot_general(
        left, right, (((1,), (1,)), ((), ())), preferred_element_type=jnp.float32
    )


def quarter_bits():
    quarter = lax.axis_index("ep") % 4
    return quarter // 2, quarter % 2


def pick(flag, when_set, when_clear):
    return jax.tree.map(lambda a, b: jnp.where(flag == 1, a, b), when_set, when_clear)


def scatter_sum(partials):
    high, low = quarter_bits()
    grouped = [p.reshape(2, 2, p.shape[0] // 4, p.shape[1]) for p in partials]
    keep_pair = pick(low, [g[:, 1] for g in grouped], [g[:, 0] for g in grouped])
    give_pair = pick(low, [g[:, 0] for g in grouped], [g[:, 1] for g in grouped])
    pair_sum = jax.tree.map(
        lambda a, b: a.astype(jnp.float32) + b.astype(jnp.float32),
        keep_pair,
        partner(give_pair, "ep", 0),
    )
    keep_group = pick(high, [p[1] for p in pair_sum], [p[0] for p in pair_sum])
    give_group = pick(high, [p[0] for p in pair_sum], [p[1] for p in pair_sum])
    return jax.tree.map(jnp.add, keep_group, partner(give_group, "ep", 1))


def gather_groups(blocks):
    high, low = quarter_bits()
    pair = jax.tree.map(lambda b, o: jnp.stack([b, o]), blocks, partner(blocks, "ep", 1))
    held = jax.tree.map(lambda b, o: jnp.stack([b, o], axis=1), pair, partner(pair, "ep", 0))
    held = pick(high, [h[::-1] for h in held], held)
    held = pick(low, [h[:, ::-1] for h in held], held)
    return [h.reshape(-1, h.shape[-1]) for h in held]


def forward_expert(row_block, w_gate, w_up, w_down):
    gate_part = jnp.dot(row_block, w_gate, preferred_element_type=jnp.float32).astype(jnp.bfloat16)
    up_part = jnp.dot(row_block, w_up, preferred_element_type=jnp.float32).astype(jnp.bfloat16)
    gate_value, up_value = scatter_sum([gate_part, up_part])
    hidden = (jax.nn.silu(gate_value) * up_value).astype(jnp.bfloat16)
    (hidden,) = gather_groups([hidden])
    return jnp.dot(hidden, w_down, preferred_element_type=jnp.float32).astype(jnp.bfloat16)


def backward_expert(row_block, grad_block, w_gate, w_up, w_down):
    gate_part = jnp.dot(row_block, w_gate, preferred_element_type=jnp.float32).astype(jnp.bfloat16)
    up_part = jnp.dot(row_block, w_up, preferred_element_type=jnp.float32).astype(jnp.bfloat16)
    grad_part = contract_cols(grad_block, w_down).astype(jnp.bfloat16)
    gate_value, up_value, grad_hidden = scatter_sum([gate_part, up_part, grad_part])
    sigmoid_value = jax.nn.sigmoid(gate_value)
    grad_gate = (
        grad_hidden * up_value * sigmoid_value * (1.0 + gate_value * (1.0 - sigmoid_value))
    ).astype(jnp.bfloat16)
    grad_up = (grad_hidden * gate_value * sigmoid_value).astype(jnp.bfloat16)
    grad_gate, grad_up = gather_groups([grad_gate, grad_up])
    result = contract_cols(grad_gate, w_gate) + contract_cols(grad_up, w_up)
    return result.astype(jnp.bfloat16)


def flip_bits(left, right, count):
    total = 0
    weight = 1
    while weight < count:
        total = total + ((left // weight + right // weight) % 2) * weight
        weight *= 2
    return total


def return_kernel(pp_count, ep_count, fwd_ref, bwd_ref, fwd_out, bwd_out, send_sem, recv_sem):
    stage = lax.axis_index("pp")
    me = lax.axis_index("ep")
    has_next = stage < pp_count - 1
    has_prev = stage > 0
    mesh_ids = pl.DeviceIdType.MESH
    barrier = pltpu.get_barrier_semaphore()

    def greet(target):
        @pl.loop(0, ep_count)
        def _(n):
            pl.semaphore_signal(barrier, 1, device_id=(target, n), device_id_type=mesh_ids)

    pl.when(has_next)(lambda: greet(stage + 1))
    pl.when(has_prev)(lambda: greet(stage - 1))
    pl.when(has_next & has_prev)(lambda: pl.semaphore_wait(barrier, 2 * ep_count))
    pl.when(jnp.logical_not(has_next & has_prev))(lambda: pl.semaphore_wait(barrier, ep_count))

    def fwd_copy(n, sender):
        return pltpu.make_async_remote_copy(
            src_ref=fwd_ref.at[n],
            dst_ref=fwd_out.at[sender],
            send_sem=send_sem.at[0, n],
            recv_sem=recv_sem.at[0, sender],
            device_id=(stage + 1, n),
            device_id_type=mesh_ids,
        )

    def bwd_copy(n, sender):
        return pltpu.make_async_remote_copy(
            src_ref=bwd_ref.at[n],
            dst_ref=bwd_out.at[sender],
            send_sem=send_sem.at[1, n],
            recv_sem=recv_sem.at[1, sender],
            device_id=(stage - 1, n),
            device_id_type=mesh_ids,
        )

    def each(body):
        @pl.loop(0, ep_count)
        def _(step):
            body(flip_bits(me, step, ep_count))

    def start_both(n):
        pl.when(has_next)(lambda: fwd_copy(n, me).start())
        pl.when(has_prev)(lambda: bwd_copy(n, me).start())

    each(start_both)
    pl.when(has_next)(lambda: each(lambda n: fwd_copy(n, me).wait_send()))
    pl.when(has_prev)(lambda: each(lambda n: bwd_copy(n, me).wait_send()))
    pl.when(has_prev)(lambda: each(lambda j: fwd_copy(me, j).wait_recv()))
    pl.when(has_next)(lambda: each(lambda j: bwd_copy(me, j).wait_recv()))


def send_back(out_fwd, out_bwd):
    pp_count = lax.axis_size("pp")
    ep_count = lax.axis_size("ep")
    chunk = jax.ShapeDtypeStruct(out_fwd.shape, out_fwd.dtype)
    return pl.pallas_call(
        functools.partial(return_kernel, pp_count, ep_count),
        out_shape=(chunk, chunk),
        in_specs=[pl.BlockSpec(memory_space=pl.ANY)] * 2,
        out_specs=(pl.BlockSpec(memory_space=pl.ANY), pl.BlockSpec(memory_space=pl.ANY)),
        scratch_shapes=[
            pltpu.SemaphoreType.DMA((2, ep_count)),
            pltpu.SemaphoreType.DMA((2, ep_count)),
        ],
        compiler_params=pltpu.CompilerParams(collective_id=0, has_side_effects=True),
    )(out_fwd, out_bwd)


def on_device(
    fwd_tokens,
    fwd_routes,
    fwd_gates,
    bwd_tokens,
    bwd_grads,
    bwd_routes,
    bwd_gates,
    gate_proj,
    up_proj,
    down_proj,
):
    expert_count = lax.axis_size("ep") // 4
    tokens_fwd = fwd_tokens[0]
    tok_count = tokens_fwd.shape[0]
    route_width = fwd_routes.shape[2]
    slot_cap = 3 * tok_count * route_width // (2 * expert_count)
    places_fwd = slot_places(fwd_routes[0], expert_count, slot_cap)
    places_bwd = slot_places(bwd_routes[0], expert_count, slot_cap)
    send_fwd = device_rows(spread_rows(places_fwd, tokens_fwd))
    send_rows = device_rows(spread_rows(places_bwd, bwd_tokens[0]))
    slot_gate = jnp.einsum("tkec,tk->ec", places_bwd, bwd_gates[0], precision=lax.Precision.HIGHEST)
    send_grads = device_rows(spread_rows(places_bwd, bwd_grads[0]) * slot_gate[:, None, :, None])
    slot_cap_fwd = send_fwd.shape[1]
    received = lax.all_to_all(
        jnp.concatenate([send_fwd, send_rows, send_grads], axis=1),
        "ep",
        split_axis=0,
        concat_axis=0,
        tiled=True,
    )
    recv_fwd = received[:, :slot_cap_fwd]
    recv_rows = received[:, slot_cap_fwd : 2 * slot_cap_fwd]
    recv_grads = received[:, 2 * slot_cap_fwd :]
    quarter_width = send_fwd.shape[2]
    w_gate = gate_proj[0, 0]
    w_up = up_proj[0, 0]
    w_down = down_proj[0, 0]
    out_fwd = forward_expert(recv_fwd.reshape(-1, quarter_width), w_gate, w_up, w_down).reshape(
        recv_fwd.shape
    )
    out_bwd = backward_expert(
        recv_rows.reshape(-1, quarter_width),
        recv_grads.reshape(-1, quarter_width),
        w_gate,
        w_up,
        w_down,
    ).reshape(recv_rows.shape)
    back_fwd, back_bwd = send_back(out_fwd, out_bwd)
    stage = lax.axis_index("pp")
    pp_count = lax.axis_size("pp")
    routes_prev = shifted(fwd_routes, "pp", 1)
    gates_prev = shifted(fwd_gates, "pp", 1)
    routes_next = shifted(bwd_routes, "pp", -1)
    places_prev = slot_places(routes_prev[0], expert_count, slot_cap)
    places_next = slot_places(routes_next[0], expert_count, slot_cap)
    gathered = collect(places_prev, back_fwd)
    mixture = (
        jnp.sum(gathered * gates_prev[0][:, :, None, None], axis=1)
        .reshape(tok_count, -1)
        .astype(jnp.bfloat16)
    )
    grad_input = (
        jnp.sum(collect(places_next, back_bwd), axis=1).reshape(tok_count, -1).astype(jnp.bfloat16)
    )
    handed_forward = jnp.where(stage == 0, jnp.zeros_like(mixture), mixture)[None]
    handed_backward = jnp.where(stage == pp_count - 1, jnp.zeros_like(grad_input), grad_input)[None]
    return (handed_forward, handed_backward)


def solution(mesh):
    return jax.shard_map(
        on_device,
        mesh=mesh,
        in_specs=(
            P("pp", "ep", None),
            P("pp", "ep", None),
            P("pp", "ep", None),
            P("pp", "ep", None),
            P("pp", "ep", None),
            P("pp", "ep", None),
            P("pp", "ep", None),
            P("pp", "ep", None, None),
            P("pp", "ep", None, None),
            P("pp", "ep", None, None),
        ),
        out_specs=(P("pp", "ep", None), P("pp", "ep", None)),
        check_vma=False,
    )
```

```python
import functools

import jax
import jax.numpy as jnp
from jax import lax
from jax.sharding import PartitionSpec as P
from jax.experimental import pallas as pl
from jax.experimental.pallas import tpu as pltpu


def partner(block, axis, distance):
    count = lax.axis_size(axis)
    route = []
    for low in range(count):
        high = low | 1 << distance
        if high != low and high < count:
            route += [(low, high), (high, low)]
    return lax.ppermute(block, axis, route)


def shifted(shard, axis, by):
    count = lax.axis_size(axis)
    pairs = [(i, i + by) for i in range(count) if 0 <= i + by < count]
    return lax.ppermute(shard, axis, pairs)


def slot_places(routes, expert_count, slot_cap):
    tok_count = routes.shape[0]
    route_width = routes.shape[1]
    flat_routes = routes.reshape(-1)
    onehot = (flat_routes[:, None] == jnp.arange(expert_count, dtype=jnp.int32)[None, :]).astype(
        jnp.int32
    )
    before = jnp.cumsum(onehot, axis=0) - onehot
    position = jnp.sum(before * onehot, axis=1)
    slot_match = (position[:, None] == jnp.arange(slot_cap, dtype=jnp.int32)[None, :]).astype(
        jnp.float32
    )
    placed = onehot.astype(jnp.float32)[:, :, None] * slot_match[:, None, :]
    return placed.reshape(tok_count, route_width, expert_count, slot_cap)


def spread_rows(places, values):
    tok_count = values.shape[0]
    quarter_width = values.shape[1] // 4
    return jnp.einsum(
        "tkec,thf->ehcf",
        places.astype(jnp.bfloat16),
        values.reshape(tok_count, 4, quarter_width),
        preferred_element_type=jnp.float32,
    )


def device_rows(placed):
    return placed.astype(jnp.bfloat16).reshape(
        4 * placed.shape[0], placed.shape[2], placed.shape[3]
    )


def collect(places, returned):
    expert_count = places.shape[2]
    shaped = returned.reshape(expert_count, 4, returned.shape[1], returned.shape[2])
    return jnp.einsum(
        "tkec,ehcf->tkhf", places.astype(jnp.bfloat16), shaped, preferred_element_type=jnp.float32
    )


def contract_cols(left, right):
    return lax.dot_general(
        left, right, (((1,), (1,)), ((), ())), preferred_element_type=jnp.float32
    )


def quarter_bits():
    quarter = lax.axis_index("ep") % 4
    return quarter // 2, quarter % 2


def pick(flag, when_set, when_clear):
    return jax.tree.map(lambda a, b: jnp.where(flag == 1, a, b), when_set, when_clear)


def scatter_sum(partials):
    high, low = quarter_bits()
    grouped = [p.reshape(2, 2, p.shape[0] // 4, p.shape[1]) for p in partials]
    keep_pair = pick(low, [g[:, 1] for g in grouped], [g[:, 0] for g in grouped])
    give_pair = pick(low, [g[:, 0] for g in grouped], [g[:, 1] for g in grouped])
    pair_sum = jax.tree.map(
        lambda a, b: a.astype(jnp.float32) + b.astype(jnp.float32),
        keep_pair,
        partner(give_pair, "ep", 0),
    )
    keep_group = pick(high, [p[1] for p in pair_sum], [p[0] for p in pair_sum])
    give_group = pick(high, [p[0] for p in pair_sum], [p[1] for p in pair_sum])
    return jax.tree.map(jnp.add, keep_group, partner(give_group, "ep", 1))


def gather_groups(blocks):
    high, low = quarter_bits()
    pair = jax.tree.map(lambda b, o: jnp.stack([b, o]), blocks, partner(blocks, "ep", 1))
    held = jax.tree.map(lambda b, o: jnp.stack([b, o], axis=1), pair, partner(pair, "ep", 0))
    held = pick(high, [h[::-1] for h in held], held)
    held = pick(low, [h[:, ::-1] for h in held], held)
    return [h.reshape(-1, h.shape[-1]) for h in held]


def forward_expert(row_block, w_gate, w_up, w_down):
    gate_part = jnp.dot(row_block, w_gate, preferred_element_type=jnp.float32).astype(jnp.bfloat16)
    up_part = jnp.dot(row_block, w_up, preferred_element_type=jnp.float32).astype(jnp.bfloat16)
    gate_value, up_value = scatter_sum([gate_part, up_part])
    hidden = (jax.nn.silu(gate_value) * up_value).astype(jnp.bfloat16)
    (hidden,) = gather_groups([hidden])
    return jnp.dot(hidden, w_down, preferred_element_type=jnp.float32).astype(jnp.bfloat16)


def backward_expert(row_block, grad_block, w_gate, w_up, w_down):
    gate_part = jnp.dot(row_block, w_gate, preferred_element_type=jnp.float32).astype(jnp.bfloat16)
    up_part = jnp.dot(row_block, w_up, preferred_element_type=jnp.float32).astype(jnp.bfloat16)
    grad_part = contract_cols(grad_block, w_down).astype(jnp.bfloat16)
    gate_value, up_value, grad_hidden = scatter_sum([gate_part, up_part, grad_part])
    sigmoid_value = jax.nn.sigmoid(gate_value)
    grad_gate = (
        grad_hidden * up_value * sigmoid_value * (1.0 + gate_value * (1.0 - sigmoid_value))
    ).astype(jnp.bfloat16)
    grad_up = (grad_hidden * gate_value * sigmoid_value).astype(jnp.bfloat16)
    grad_gate, grad_up = gather_groups([grad_gate, grad_up])
    result = contract_cols(grad_gate, w_gate) + contract_cols(grad_up, w_up)
    return result.astype(jnp.bfloat16)


def return_kernel(pp_count, ep_count, fwd_ref, bwd_ref, fwd_out, bwd_out, send_sem, recv_sem):
    stage = lax.axis_index("pp")
    me = lax.axis_index("ep")
    has_next = stage < pp_count - 1
    has_prev = stage > 0
    mesh_ids = pl.DeviceIdType.MESH
    barrier = pltpu.get_barrier_semaphore()

    def greet(target):
        @pl.loop(0, ep_count)
        def _(n):
            pl.semaphore_signal(barrier, 1, device_id=(target, n), device_id_type=mesh_ids)

    pl.when(has_next)(lambda: greet(stage + 1))
    pl.when(has_prev)(lambda: greet(stage - 1))
    pl.when(has_next & has_prev)(lambda: pl.semaphore_wait(barrier, 2 * ep_count))
    pl.when(jnp.logical_not(has_next & has_prev))(lambda: pl.semaphore_wait(barrier, ep_count))

    def fwd_copy(n, sender):
        return pltpu.make_async_remote_copy(
            src_ref=fwd_ref.at[n],
            dst_ref=fwd_out.at[sender],
            send_sem=send_sem.at[0, n],
            recv_sem=recv_sem.at[0, sender],
            device_id=(stage + 1, n),
            device_id_type=mesh_ids,
        )

    def bwd_copy(n, sender):
        return pltpu.make_async_remote_copy(
            src_ref=bwd_ref.at[n],
            dst_ref=bwd_out.at[sender],
            send_sem=send_sem.at[1, n],
            recv_sem=recv_sem.at[1, sender],
            device_id=(stage - 1, n),
            device_id_type=mesh_ids,
        )

    def each(body):
        @pl.loop(0, ep_count)
        def _(step):
            body(lax.rem(me + 1 + step, ep_count))

    def start_both(n):
        pl.when(has_next)(lambda: fwd_copy(n, me).start())
        pl.when(has_prev)(lambda: bwd_copy(n, me).start())

    each(start_both)
    pl.when(has_prev)(lambda: each(lambda j: fwd_copy(me, j).wait_recv()))
    pl.when(has_next)(lambda: each(lambda j: bwd_copy(me, j).wait_recv()))
    pl.when(has_next)(lambda: each(lambda n: fwd_copy(n, me).wait_send()))
    pl.when(has_prev)(lambda: each(lambda n: bwd_copy(n, me).wait_send()))


def send_back(out_fwd, out_bwd):
    pp_count = lax.axis_size("pp")
    ep_count = lax.axis_size("ep")
    chunk = jax.ShapeDtypeStruct(out_fwd.shape, out_fwd.dtype)
    return pl.pallas_call(
        functools.partial(return_kernel, pp_count, ep_count),
        out_shape=(chunk, chunk),
        in_specs=[pl.BlockSpec(memory_space=pl.ANY)] * 2,
        out_specs=(pl.BlockSpec(memory_space=pl.ANY), pl.BlockSpec(memory_space=pl.ANY)),
        scratch_shapes=[
            pltpu.SemaphoreType.DMA((2, ep_count)),
            pltpu.SemaphoreType.DMA((2, ep_count)),
        ],
        compiler_params=pltpu.CompilerParams(collective_id=0, has_side_effects=True),
    )(out_fwd, out_bwd)


def on_device(
    fwd_tokens,
    fwd_routes,
    fwd_gates,
    bwd_tokens,
    bwd_grads,
    bwd_routes,
    bwd_gates,
    gate_proj,
    up_proj,
    down_proj,
):
    expert_count = lax.axis_size("ep") // 4
    tokens_fwd = fwd_tokens[0]
    tok_count = tokens_fwd.shape[0]
    route_width = fwd_routes.shape[2]
    slot_cap = 3 * tok_count * route_width // (2 * expert_count)
    places_fwd = slot_places(fwd_routes[0], expert_count, slot_cap)
    places_bwd = slot_places(bwd_routes[0], expert_count, slot_cap)
    send_fwd = device_rows(spread_rows(places_fwd, tokens_fwd))
    send_rows = device_rows(spread_rows(places_bwd, bwd_tokens[0]))
    slot_gate = jnp.einsum("tkec,tk->ec", places_bwd, bwd_gates[0], precision=lax.Precision.HIGHEST)
    send_grads = device_rows(spread_rows(places_bwd, bwd_grads[0]) * slot_gate[:, None, :, None])
    slot_cap_fwd = send_fwd.shape[1]
    received = lax.all_to_all(
        jnp.concatenate([send_fwd, send_rows, send_grads], axis=1),
        "ep",
        split_axis=0,
        concat_axis=0,
        tiled=True,
    )
    recv_fwd = received[:, :slot_cap_fwd]
    recv_rows = received[:, slot_cap_fwd : 2 * slot_cap_fwd]
    recv_grads = received[:, 2 * slot_cap_fwd :]
    quarter_width = send_fwd.shape[2]
    w_gate = gate_proj[0, 0]
    w_up = up_proj[0, 0]
    w_down = down_proj[0, 0]
    out_fwd = forward_expert(recv_fwd.reshape(-1, quarter_width), w_gate, w_up, w_down).reshape(
        recv_fwd.shape
    )
    out_bwd = backward_expert(
        recv_rows.reshape(-1, quarter_width),
        recv_grads.reshape(-1, quarter_width),
        w_gate,
        w_up,
        w_down,
    ).reshape(recv_rows.shape)
    back_fwd, back_bwd = send_back(out_fwd, out_bwd)
    stage = lax.axis_index("pp")
    pp_count = lax.axis_size("pp")
    routes_prev = shifted(fwd_routes, "pp", 1)
    gates_prev = shifted(fwd_gates, "pp", 1)
    routes_next = shifted(bwd_routes, "pp", -1)
    places_prev = slot_places(routes_prev[0], expert_count, slot_cap)
    places_next = slot_places(routes_next[0], expert_count, slot_cap)
    gathered = collect(places_prev, back_fwd)
    mixture = (
        jnp.sum(gathered * gates_prev[0][:, :, None, None], axis=1)
        .reshape(tok_count, -1)
        .astype(jnp.bfloat16)
    )
    grad_input = (
        jnp.sum(collect(places_next, back_bwd), axis=1).reshape(tok_count, -1).astype(jnp.bfloat16)
    )
    handed_forward = jnp.where(stage == 0, jnp.zeros_like(mixture), mixture)[None]
    handed_backward = jnp.where(stage == pp_count - 1, jnp.zeros_like(grad_input), grad_input)[None]
    return (handed_forward, handed_backward)


def solution(mesh):
    return jax.shard_map(
        on_device,
        mesh=mesh,
        in_specs=(
            P("pp", "ep", None),
            P("pp", "ep", None),
            P("pp", "ep", None),
            P("pp", "ep", None),
            P("pp", "ep", None),
            P("pp", "ep", None),
            P("pp", "ep", None),
            P("pp", "ep", None, None),
            P("pp", "ep", None, None),
            P("pp", "ep", None, None),
        ),
        out_specs=(P("pp", "ep", None), P("pp", "ep", None)),
        check_vma=False,
    )
```
